32 devices in a mesh: parts: 2 (over y), tm: 16 (over z, x, core).
Axes of the slice: x: 2, y: 2, z: 4, core: 2. Of those that a mesh axis runs over, the one named last changes fastest.
Arguments:
- signal: bfloat16 [16384, 1024], P(('parts', 'tm')), parts along dimension 0, may hold values from -6 to 6
- pool_weight: bfloat16 [4096, 2048], P('tm'), may hold values from -0.09375 to 0.09375
- norm_gain: float32 [2, 2048], replicated, may hold values from 0.1 to 1.9
- step_size: float32 [2, 2048], replicated, may hold values from 0 to 0.05, as said below
- mode_out: float32 [2, 32, 2048], replicated, may hold values from -1 to 1
- skip_gain: float32 [2, 2048], replicated, may hold values from -4 to 4
Outputs:
- pooled_out: bfloat16 [4096, 2048], P(('parts', 'tm')), parts along dimension 0
The draws below stay inside these ranges and needn't reach their ends.
There are 2 independent parts, one for each index of `parts`. The reference program is written for one: setup_inputs(seed, part) draws one part's arguments, and reference() takes and returns one part's arrays. A program takes and returns all parts, laid end to end along the dimension named above; an argument that names none is the same for every part. Nothing has to cross between parts.
Inputs may be any that keep to these rules, and one draw needn't show every extreme that they name: `step_size`: positive step sizes.
All inputs are finite; a program needn't handle non-finite values.
Results may differ from the reference program's by a relative error of at most 0.001.
Values may be sent and summed in bfloat16 or wider, within the bound.
A program may use at most 320 MiB of HBM per device.

```python
import jax
import jax.numpy as jnp
from jax import lax

CIN = 1024
H = 2048
NS = 32
POOL = 4
LAYERS = 2
SEQ = 2048
FINE = 8192


def draw_step_size(key, part):
    pick_key, slow_key, fast_key = jax.random.split(key, 3)
    slow_share = 0.5
    slow_low = 0.3
    slow_high = 3.0
    slow_pick = jax.random.bernoulli(pick_key, slow_share, (LAYERS, H))
    slow_steps = jnp.exp(jax.random.uniform(slow_key, (LAYERS, H), jnp.float32, jnp.log(slow_low), jnp.log(slow_high))) / SEQ
    fast_steps = jnp.exp(jax.random.uniform(fast_key, (LAYERS, H), jnp.float32, jnp.log(1.0 / 48.0), jnp.log(1.0 / 24.0)))
    return jnp.where(slow_pick, slow_steps, fast_steps).astype(jnp.float32)


def level_of(own_key, dims, cuts, least, largest):
    def one(axis_at, blocks):
        heights = jax.random.uniform(jax.random.fold_in(jax.random.fold_in(own_key, 6), axis_at), (blocks,), jnp.float32, least / len(cuts), largest / len(cuts))
        return jnp.repeat(jnp.exp(heights), dims[axis_at] // blocks).reshape((-1,) + (1,) * (len(dims) - axis_at - 1))

    gain = one(*cuts[0])
    for cut in cuts[1:]:
        gain = gain * one(*cut)
    return gain


def bell_draw(own_key, dims, deviation, bound, cuts=(), held_as=jnp.bfloat16):
    gain = level_of(own_key, dims, cuts, -0.22, 0.18) if cuts else 1.0
    entries = jax.random.normal(own_key, dims, jnp.float32) * deviation * gain
    return jnp.minimum(jnp.maximum(entries, -bound), bound).astype(held_as)


def setup_inputs(seed: int = 0, part: int = 0) -> dict:
    splits = jax.random.split(jax.random.key(seed), 7)
    part_splits = jax.random.split(jax.random.fold_in(splits[6], part), 7)
    signal = bell_draw(part_splits[0], (FINE, CIN), 1.0, 6.0, ((0, 16),))
    pool_weight = bell_draw(splits[1], (POOL * CIN, H), (POOL * CIN) ** -0.5, 0.09375, ((0, 16),))
    norm_gain = jnp.clip(1.0 + 0.18 * jax.random.normal(splits[2], (LAYERS, H), jnp.float32), 0.1, 1.9)
    step_size = draw_step_size(jax.random.fold_in(splits[6], 71), part)
    mode_out = bell_draw(splits[4], (LAYERS, NS, H), NS ** -0.5, 1.0, (), jnp.float32)
    skip_gain = bell_draw(splits[5], (LAYERS, H), 1.0, 4.0, (), jnp.float32)
    return {"signal": signal, "pool_weight": pool_weight, "norm_gain": norm_gain, "step_size": step_size, "mode_out": mode_out, "skip_gain": skip_gain}


def build_tables(decay_rates, in_scale, out_mix, block_len):
    lag_steps = jnp.arange(block_len, dtype=jnp.float32)
    powers = jnp.exp(-lag_steps[:, None, None] * decay_rates[None])
    kernel = lax.optimization_barrier(jnp.sum(out_mix[None] * in_scale[None] * powers, axis=1))
    lag_index = jnp.arange(block_len, dtype=jnp.int32)
    lag_gap = lag_index[:, None] - lag_index[None, :]
    picked = kernel[jnp.clip(lag_gap, 0, block_len - 1).astype(jnp.int32)]
    toeplitz = jnp.where((lag_gap >= 0)[:, :, None], picked, jnp.zeros_like(picked))
    into_table = in_scale[None] * jnp.exp(-(block_len - 1 - lag_steps)[:, None, None] * decay_rates[None])
    outof_table = out_mix[None] * jnp.exp(-(lag_steps + 1.0)[:, None, None] * decay_rates[None])
    return (toeplitz, into_table, outof_table)

def layer_norm(hidden, gain_row):
    row_mean = lax.optimization_barrier(jnp.mean(hidden, axis=-1, keepdims=True))
    centered = hidden - row_mean
    row_var = lax.optimization_barrier(jnp.mean(centered * centered, axis=-1, keepdims=True))
    return centered * lax.rsqrt(row_var + 1e-05) * gain_row[None, :]

def state_layer(hidden, gain_row, step_row, out_mix, skip_row):
    row_count, chan_count = hidden.shape
    modes = out_mix.shape[0]
    block_len = min(64, row_count)
    blocks = row_count // block_len
    normed = layer_norm(hidden, gain_row)
    decay_rates = step_row[None, :] * (jnp.arange(modes, dtype=jnp.float32) + 1.0)[:, None]
    in_scale = jnp.sqrt(-jnp.expm1(-2.0 * decay_rates))
    toeplitz, into_table, outof_table = build_tables(decay_rates, in_scale, out_mix, block_len)
    block_decay = jnp.exp(-decay_rates * block_len)
    exact = lax.Precision.HIGHEST
    grouped = normed.reshape(blocks, block_len, chan_count)

    def advance(state, block_rows):
        inner = jnp.einsum('tsh,sh->th', toeplitz, block_rows, precision=exact)
        carried = jnp.einsum('tnh,nh->th', outof_table, state, precision=exact)
        response = inner + carried + skip_row[None, :] * block_rows
        new_state = block_decay * state + jnp.einsum('snh,sh->nh', into_table, block_rows, precision=exact)
        return (new_state, response)
    start_state = jnp.zeros((modes, chan_count), jnp.float32)
    final_state, responses = lax.scan(advance, start_state, grouped)
    response = responses.reshape(row_count, chan_count)
    return hidden + jax.nn.gelu(response, approximate=False)

def reference(signal, pool_weight, norm_gain, step_size, mode_out, skip_gain):
    coarse = signal.reshape(SEQ, POOL * CIN)
    hidden = jnp.dot(coarse, pool_weight, preferred_element_type=jnp.float32)
    for layer_index in range(LAYERS):
        hidden = state_layer(hidden, norm_gain[layer_index], step_size[layer_index], mode_out[layer_index], skip_gain[layer_index])
    return hidden.astype(jnp.bfloat16)
```

```python
import functools

import jax
import jax.numpy as jnp
from jax import lax
from jax.experimental import pallas as pl
from jax.experimental.pallas import tpu as pltpu
from jax.sharding import PartitionSpec as P

POOL = 4
SPLIT = 4
BLOCK = 16
LANES = 128
PIECES = 4
PAD = 1


def block_ends(x_ref, decay_ref, ends_ref, modes, cols):
    rows = x_ref.shape[0]
    blocks = rows // BLOCK
    span = 8 * BLOCK
    pitch = ends_ref.shape[0] // blocks

    def group(g, carry):
        base = pl.multiple_of(g * span, span)
        xs = [x_ref[pl.ds(base + j, 8, stride=BLOCK), cols] for j in range(BLOCK)]
        for n in range(modes):
            decay = jnp.broadcast_to(decay_ref[pl.ds(n, 1), cols], (8, LANES))
            end = xs[0]
            for j in range(1, BLOCK):
                end = end * decay + xs[j]
            ends_ref[pl.ds(g * 8 * pitch + n, 8, stride=pitch), cols] = end
        return carry

    lax.fori_loop(0, rows // span, group, 0)


def scan_blocks(blocks, ends_ref, step_ref, modes, cols, start, out_ref=None):
    pitch = ends_ref.shape[0] // blocks
    groups = modes // 8
    steps = [step_ref[pl.ds(i * 8, 8), cols] for i in range(groups)]
    outs = [out_ref[pl.ds(i * 8, 8), cols] for i in range(groups)] if out_ref is not None else None
    states = list(start)
    for b in range(blocks):
        for i in range(groups):
            where = pl.ds(b * pitch + i * 8, 8)
            end = ends_ref[where, cols]
            if outs is not None:
                ends_ref[where, cols] = states[i] * outs[i]
            states[i] = states[i] * steps[i] + end
    return states


def respond(x_ref, hidden_ref, ends_ref, powers_ref, kernel_ref, result_ref, modes, cols):
    rows = x_ref.shape[0]
    blocks = rows // BLOCK
    span = 8 * BLOCK
    pitch = ends_ref.shape[0] // blocks

    def group(g, carry):
        base = pl.multiple_of(g * span, span)
        coefs = [ends_ref[pl.ds(g * 8 * pitch + n, 8, stride=pitch), cols] for n in range(modes)]
        xs = [x_ref[pl.ds(base + j, 8, stride=BLOCK), cols] for j in range(BLOCK)]
        for j in range(BLOCK):
            power = jnp.broadcast_to(powers_ref[pl.ds(j, 1), cols], (8, LANES))
            total = coefs[modes - 1]
            for n in range(modes - 2, -1, -1):
                total = total * power + coefs[n]
            total = total * power
            for i in range(j + 1):
                total = total + xs[i] * jnp.broadcast_to(
                    kernel_ref[pl.ds(j - i, 1), cols], (8, LANES)
                )
            where = pl.ds(base + j, 8, stride=BLOCK)
            gelu = 0.5 * total * (1.0 + lax.erf(total * 0.7071067811865476))
            result_ref[where, cols] = hidden_ref[where, cols] + gelu
        return carry

    lax.fori_loop(0, rows // span, group, 0)


MESH = pl.DeviceIdType.MESH


def pool_kernel(highs, coarse_ref, weight_ref, hidden_ref, all_ref, cols_ref, sems):
    part, place = lax.axis_index("parts"), lax.axis_index("tm")
    high, low = place // SPLIT, place % SPLIT
    depth, width = weight_ref.shape[0], cols_ref.shape[1]
    half = depth // 2
    rows = coarse_ref.shape[0]
    piece = rows // PIECES
    chunk = SPLIT * depth
    other = 1 - part
    (near_send, near_recv, own_sem, line_send, line_recv, side_send, side_recv,
     rows_send, rows_recv) = sems
    flip = lambda bit: low + bit - 2 * bit * ((low // bit) % 2)
    core, cross = flip(1), flip(2)
    diagonal = SPLIT - 1 - low
    at = lambda p, h, l: (p, h * SPLIT + l)

    barrier = pltpu.get_barrier_semaphore()

    def greet(device):
        pl.semaphore_signal(barrier, inc=1, device_id=device, device_id_type=MESH)

    for who in (core, cross, diagonal):
        greet(at(part, high, who))
    greet(at(other, high, low))
    pl.when(high > 0)(lambda: greet(at(part, high - 1, low)))
    pl.when(high < highs - 1)(lambda: greet(at(part, high + 1, low)))

    def spot(h, l, which):
        start = pl.multiple_of(h * chunk + l * depth + which * half, half)
        return cols_ref.at[pl.ds(start, half), :]

    def near(bit, which):
        to = (core, cross, diagonal)[bit]
        mine = weight_ref.at[
            pl.ds(pl.multiple_of(which * half, half), half),
            pl.ds(pl.multiple_of(to * width, width), width),
        ]
        return pltpu.make_async_remote_copy(
            mine, spot(high, low, which), near_send.at[bit, which], near_recv.at[bit, which],
            device_id=at(part, high, to), device_id_type=MESH,
        )

    def near_arrived(bit, which):
        who = (core, cross, diagonal)[bit]
        pltpu.make_async_remote_copy(
            spot(high, who, which), spot(high, who, which), near_send.at[bit, which],
            near_recv.at[bit, which], device_id=at(part, high, who), device_id_type=MESH,
        ).wait_recv()

    def line(up, h, l):
        to = jnp.clip(high + (1 if up else -1), 0, highs - 1)
        return pltpu.make_async_remote_copy(
            spot(h, l, part), spot(h, l, part), line_send.at[int(up), h, l], line_recv.at[h, l],
            device_id=at(part, to, low), device_id_type=MESH,
        )

    def side(h, l, which):
        return pltpu.make_async_remote_copy(
            spot(h, l, which), spot(h, l, which), side_send.at[h, l], side_recv.at[h, l],
            device_id=at(other, high, low), device_id_type=MESH,
        )

    def block(owner, p):
        start = pl.multiple_of(owner * rows + p * piece, piece)
        return all_ref.at[pl.ds(start, piece), :]

    def give(bit, p):
        to = core if bit == 0 else cross
        return pltpu.make_async_remote_copy(
            coarse_ref.at[pl.ds(p * piece, piece), :], block(low, p), rows_send.at[bit, p],
            rows_recv.at[bit, p], device_id=at(part, high, to), device_id_type=MESH,
        )

    def taken(bit, p):
        who = (core, cross, diagonal)[bit]
        pltpu.make_async_remote_copy(
            block(who, p), block(who, p), rows_send.at[bit, p], rows_recv.at[bit, p],
            device_id=at(part, high, core), device_id_type=MESH,
        ).wait_recv()

    def pass_on(p):
        return pltpu.make_async_remote_copy(
            block(cross, p), block(cross, p), rows_send.at[2, p], rows_recv.at[2, p],
            device_id=at(part, high, core), device_id_type=MESH,
        )

    own_weight = pltpu.make_async_copy(
        weight_ref.at[:, pl.ds(pl.multiple_of(low * width, width), width)],
        cols_ref.at[pl.ds(pl.multiple_of(high * chunk + low * depth, depth), depth), :],
        own_sem.at[0],
    )
    own_rows = pltpu.make_async_copy(
        coarse_ref, all_ref.at[pl.ds(pl.multiple_of(low * rows, rows), rows), :], own_sem.at[1]
    )
    own_weight.start()
    own_rows.start()
    ahead = jnp.minimum(high, 1) + jnp.minimum(highs - 1 - high, 1)
    pl.semaphore_wait(barrier, 4 + ahead)

    for bit in (1, 2, 0):
        near(bit, part).start()
    for p in range(PIECES):
        give(1, p).start()
    for p in range(PIECES):
        give(0, p).start()
    for bit in (1, 2, 0):
        near(bit, other).start()

    def both_ways(h, l):
        pl.when(high < highs - 1)(lambda: line(True, h, l).start())
        pl.when(high > 0)(lambda: line(False, h, l).start())

    own_weight.wait()
    both_ways(high, low)
    for bit, who in ((0, core), (1, cross), (2, diagonal)):
        near_arrived(bit, part)
        both_ways(high, who)

    def relay(s, l):
        @pl.when(high - s >= 0)
        def _():
            h = high - s
            line(True, h, l).wait_recv()
            pl.when(high < highs - 1)(lambda: line(True, h, l).start())
            side(h, l, part).start()

        @pl.when(high + s < highs)
        def _():
            h = high + s
            line(False, h, l).wait_recv()
            pl.when(high > 0)(lambda: line(False, h, l).start())
            side(h, l, part).start()

    def step(s, carry):
        for l in (low, core, cross, diagonal):
            relay(s, l)

        @pl.when(s < PIECES)
        def _():
            taken(1, s - 1)
            pass_on(s - 1).start()

        return carry

    last = highs - 1
    lax.fori_loop(1, last, step, 0)
    for l in (low, core, cross):
        relay(last, l)
    for p in range(min(PIECES - 1, last - 1), PIECES):
        taken(1, p)
        pass_on(p).start()
    own_rows.wait()
    for p in range(PIECES):
        taken(0, p)
        taken(2, p)
    for bit in range(3):
        near_arrived(bit, other)

    def multiply(h):
        start = pl.multiple_of(h * chunk, chunk)
        return jnp.dot(
            all_ref[:, pl.ds(start, chunk)], cols_ref[pl.ds(start, chunk), :],
            preferred_element_type=jnp.float32,
        )

    def keep(value, first):
        for g in range(width // LANES):
            piece_of = value[:, g * LANES : (g + 1) * LANES]
            hidden_ref[g] = piece_of if first else hidden_ref[g] + piece_of

    keep(multiply(high), True)

    def add(s, carry):
        for h, there in ((high - s, high - s >= 0), (high + s, high + s < highs)):
            @pl.when(there)
            def _(h=h):
                for l in range(SPLIT):
                    side(h, l, other).wait_recv()
                keep(multiply(h), False)

        return carry

    lax.fori_loop(1, last, add, 0)
    relay(last, diagonal)
    add(last, 0)

    for bit in range(3):
        near(bit, 0).wait_send()
        near(bit, 1).wait_send()
    for p in range(PIECES):
        give(0, p).wait_send()
        give(1, p).wait_send()
        pass_on(p).wait_send()

    def sent(h, carry):
        for l in range(SPLIT):
            pl.when((h <= high) & (high < highs - 1))(lambda: line(True, h, l).wait_send())
            pl.when((h >= high) & (high > 0))(lambda: line(False, h, l).wait_send())
            pl.when(h != high)(lambda: side(h, l, part).wait_send())
        return carry

    lax.fori_loop(0, highs, sent, 0)


def pool(coarse, weight):
    rows, features = coarse.shape
    width = weight.shape[1] // SPLIT
    highs = lax.axis_size("tm") // SPLIT
    dma = pltpu.SemaphoreType.DMA
    vmem = pl.BlockSpec(memory_space=pltpu.VMEM)
    return pl.pallas_call(
        functools.partial(pool_kernel, highs),
        out_shape=jax.ShapeDtypeStruct((width // LANES, rows * SPLIT, LANES), jnp.float32),
        in_specs=[vmem, vmem],
        out_specs=vmem,
        scratch_shapes=[
            pltpu.VMEM((rows * SPLIT, features), jnp.bfloat16),
            pltpu.VMEM((features, width), jnp.bfloat16),
            [
                dma((3, 2)), dma((3, 2)), dma((2,)), dma((2, highs, SPLIT)), dma((highs, SPLIT)),
                dma((highs, SPLIT)), dma((highs, SPLIT)), dma((3, PIECES)), dma((3, PIECES)),
            ],
        ],
        compiler_params=pltpu.CompilerParams(collective_id=0, has_side_effects=True),
    )(coarse, weight)


def tables(step_row, out_mix, skip_row, rows):
    modes = out_mix.shape[0]
    rates = step_row[None, :] * (jnp.arange(modes, dtype=jnp.float32) + 1.0)[:, None]
    in_scale = jnp.sqrt(-jnp.expm1(-2.0 * rates))
    out = out_mix * in_scale
    lags = jnp.arange(BLOCK, dtype=jnp.float32)
    kernel = jnp.sum(out[None] * jnp.exp(-lags[:, None, None] * rates[None]), axis=1)
    kernel = kernel.at[0].add(skip_row)
    powers = jnp.exp(-(lags + 1.0)[:, None] * step_row[None, :])
    return jnp.concatenate(
        [jnp.exp(-rates), jnp.exp(-rates * BLOCK), jnp.exp(-rates * rows), out]
        + [jnp.pad(extra, ((0, modes - BLOCK), (0, 0))) for extra in (powers, kernel)]
    )


def layers_kernel(
    highs, modes, hidden_in_ref, gain_ref, table_ref, out_ref, hidden_ref, x_ref, ends_ref,
    stats_ref, last_ref, states_ref, rounded_ref, sems
):
    stats_send, stats_recv, state_send, state_recv, out_send, out_recv = sems
    part, place = lax.axis_index("parts"), lax.axis_index("tm")
    high, low = place // SPLIT, place % SPLIT
    groups, rows, _ = hidden_in_ref.shape
    chans = groups * LANES
    layers = gain_ref.shape[0]
    flip = lambda bit: low + bit - 2 * bit * ((low // bit) % 2)
    near = (flip(1), flip(2), SPLIT - 1 - low)
    at = lambda h, l: (part, h * SPLIT + l)
    own_rows = rows // SPLIT
    blocks = rows // BLOCK
    exact = lax.Precision.HIGHEST

    barrier = pltpu.get_barrier_semaphore()

    def greet(device):
        pl.semaphore_signal(barrier, inc=1, device_id=device, device_id_type=MESH)

    for who in near:
        greet(at(high, who))

    def greet_high(h, carry):
        pl.when(h != high)(lambda: greet(at(h, low)))
        return carry

    lax.fori_loop(0, highs, greet_high, 0)

    def stats_copy(l, bit, owner):
        return pltpu.make_async_remote_copy(
            stats_ref.at[l, owner], stats_ref.at[l, owner], stats_send.at[l, bit],
            stats_recv.at[l, bit], device_id=at(high, near[bit]), device_id_type=MESH,
        )

    def state_copy(l, g, source, target):
        return pltpu.make_async_remote_copy(
            last_ref.at[l, g], states_ref.at[l, source, g], state_send.at[l, target, g],
            state_recv.at[l, source, g], device_id=at(target, low), device_id_type=MESH,
        )

    def out_cols(owner, g):
        return pl.ds(pl.multiple_of(owner * chans + g * LANES, LANES), LANES)

    def out_copy(g, bit, owner):
        start = pl.multiple_of(near[bit] * own_rows, own_rows)
        return pltpu.make_async_remote_copy(
            rounded_ref.at[g, pl.ds(start, own_rows), :], out_ref.at[:, out_cols(owner, g)],
            out_send.at[g, bit], out_recv.at[g, bit],
            device_id=at(high, near[bit]), device_id_type=MESH,
        )

    for l in range(layers):
        source_ref = hidden_in_ref if l == 0 else hidden_ref
        total = source_ref[0]
        for g in range(1, groups):
            total = total + source_ref[g]
        mean = jnp.sum(total, axis=-1, keepdims=True) / chans
        square = jnp.square(source_ref[0] - mean)
        for g in range(1, groups):
            square = square + jnp.square(source_ref[g] - mean)
        ones = jnp.ones((8, LANES), jnp.float32)
        across = lambda v: lax.dot_general(
            ones, v, (((1,), (1,)), ((), ())), precision=exact, preferred_element_type=jnp.float32
        )
        line = lax.broadcasted_iota(jnp.int32, (8, rows), 0)
        stats_ref[l, low] = jnp.where(line == 0, across(total) / chans, across(square))
        if l == 0:
            pl.semaphore_wait(barrier, 3 + highs - 1)
        for bit in (1, 2, 0):
            stats_copy(l, bit, low).start()
        for bit in range(3):
            stats_copy(l, bit, near[bit]).wait_recv()
        every = [stats_ref[l, i] for i in range(SPLIT)]
        means = [e[0:1] for e in every]
        row_mean = (means[0] + means[1] + means[2] + means[3]) / SPLIT
        row_var = sum(e[1:2] + chans * jnp.square(e[0:1] - row_mean) for e in every)
        row_scale = lax.rsqrt(row_var / (chans * SPLIT) + 1e-05)
        both = jnp.where(line == 0, row_mean, row_scale)
        both = jnp.transpose(both)
        row_mean, row_scale = both[:, 0:1], both[:, 1:2]
        for g in range(groups):
            gain = gain_ref[pl.ds(l, 1), pl.ds(g * LANES, LANES)]
            x_ref[g] = (source_ref[g] - row_mean) * row_scale * gain

        def table(index, g, size):
            return table_ref.at[l, pl.ds(index * modes, size), pl.ds(pl.multiple_of(g * LANES, LANES), LANES)]

        cols = slice(None)
        eights = modes // 8

        def send(g):
            def one(h, carry):
                pl.when(h > high)(lambda: state_copy(l, g, high, h).start())
                return carry

            lax.fori_loop(1, highs, one, 0)

        def ends(g, carry):
            block_ends(x_ref.at[g], table(0, g, modes), ends_ref.at[g], modes, cols)
            zero = [jnp.zeros((8, LANES), jnp.float32)] * eights
            last = scan_blocks(blocks, ends_ref.at[g], table(1, g, modes), modes, cols, zero)
            for i in range(eights):
                last_ref[l, g, pl.ds(i * 8, 8), :] = last[i]
            send(g)
            return carry

        lax.fori_loop(0, groups, ends, 0)

        def finish(g, carry):
            whole = table(2, g, modes)

            def join(h, start):
                @pl.when(h < high)
                def _():
                    state_copy(l, g, h, high).wait_recv()
                    states_ref[l, high, g] = whole[...] * states_ref[l, high, g] + states_ref[l, h, g]
                return start

            states_ref[l, high, g] = jnp.zeros((modes, LANES), jnp.float32)
            lax.fori_loop(0, highs - 1, join, 0)
            start = [states_ref[l, high, g, pl.ds(i * 8, 8), :] for i in range(eights)]
            scan_blocks(
                blocks, ends_ref.at[g], table(1, g, modes), modes, cols, start, table(3, g, modes)
            )
            respond(
                x_ref.at[g], source_ref.at[g], ends_ref.at[g], table(4, g, BLOCK),
                table(5, g, BLOCK), hidden_ref.at[g], modes, cols,
            )
            if l == layers - 1:
                rounded_ref[g] = hidden_ref[g].astype(jnp.bfloat16)
                for bit in (1, 2, 0):
                    out_copy(g, bit, low).start()
                out_ref[:, out_cols(low, g)] = rounded_ref[
                    g, pl.ds(pl.multiple_of(low * own_rows, own_rows), own_rows), :
                ]
            return carry

        lax.fori_loop(0, groups, finish, 0)

    def drain(g, carry):
        for bit in range(3):
            out_copy(g, bit, near[bit]).wait_recv()
            out_copy(g, bit, low).wait_send()

        def one(h, carry):
            @pl.when(h > high)
            def _():
                for l in range(layers):
                    state_copy(l, g, high, h).wait_send()
            return carry

        return lax.fori_loop(1, highs, one, carry)

    lax.fori_loop(0, groups, drain, 0)
    for l in range(layers):
        for bit in range(3):
            stats_copy(l, bit, low).wait_send()


def run_layers(hidden, gain, table, modes):
    groups, rows, _ = hidden.shape
    layers = gain.shape[0]
    highs = lax.axis_size("tm") // SPLIT
    dma = pltpu.SemaphoreType.DMA
    vmem = pl.BlockSpec(memory_space=pltpu.VMEM)
    f32 = jnp.float32
    return pl.pallas_call(
        functools.partial(layers_kernel, highs, modes),
        out_shape=jax.ShapeDtypeStruct((rows // SPLIT, groups * LANES * SPLIT), jnp.bfloat16),
        in_specs=[vmem] * 3,
        out_specs=vmem,
        scratch_shapes=[
            pltpu.VMEM((groups, rows, LANES), f32),
            pltpu.VMEM((groups, rows, LANES), f32),
            pltpu.VMEM((groups, (modes + PAD) * (rows // BLOCK), LANES), f32),
            pltpu.VMEM((layers, SPLIT, 8, rows), f32),
            pltpu.VMEM((layers, groups, modes, LANES), f32),
            pltpu.VMEM((layers, highs, groups, modes, LANES), f32),
            pltpu.VMEM((groups, rows, LANES), jnp.bfloat16),
            [
                dma((layers, 3)), dma((layers, 3)), dma((layers, highs, groups)),
                dma((layers, highs, groups)), dma((groups, 3)), dma((groups, 3)),
            ],
        ],
        compiler_params=pltpu.CompilerParams(collective_id=1, has_side_effects=True),
    )(hidden, gain, table)


def local(signal, pool_weight, norm_gain, step_size, mode_out, skip_gain):
    fine_rows, channels = signal.shape
    low = lax.axis_index("tm") % SPLIT
    coarse = signal.reshape(fine_rows // POOL, POOL * channels)
    chans = pool_weight.shape[1] // SPLIT
    rows = SPLIT * coarse.shape[0]
    modes = mode_out.shape[1]

    def own(array):
        return lax.dynamic_slice_in_dim(array, low * chans, chans, axis=array.ndim - 1)

    gain, step, mix, skip = own(norm_gain), own(step_size), own(mode_out), own(skip_gain)
    table = jax.vmap(functools.partial(tables, rows=rows))(step, mix, skip)
    hidden = pool(coarse, pool_weight)
    return run_layers(hidden, gain, table, modes)


def solution(mesh):
    placed = (P(("parts", "tm"), None), P("tm", None), P(), P(), P(), P())
    return jax.shard_map(
        local, mesh=mesh, in_specs=placed, out_specs=P(("parts", "tm"), None), check_vma=False
    )
```

```python
import functools

import jax
import jax.numpy as jnp
from jax import lax
from jax.experimental import pallas as pl
from jax.experimental.pallas import tpu as pltpu
from jax.sharding import PartitionSpec as P

POOL = 4
SPLIT = 4
BLOCK = 16
LANES = 128
PIECES = 4
PAD = 1


def block_ends(x_ref, decay_ref, ends_ref, modes, cols):
    rows = x_ref.shape[0]
    blocks = rows // BLOCK
    span = 8 * BLOCK
    pitch = ends_ref.shape[0] // blocks

    def group(g, carry):
        base = pl.multiple_of(g * span, span)
        xs = [x_ref[pl.ds(base + j, 8, stride=BLOCK), cols] for j in range(BLOCK)]
        for n in range(modes):
            decay = jnp.broadcast_to(decay_ref[pl.ds(n, 1), cols], (8, LANES))
            end = xs[0]
            for j in range(1, BLOCK):
                end = end * decay + xs[j]
            ends_ref[pl.ds(g * 8 * pitch + n, 8, stride=pitch), cols] = end
        return carry

    lax.fori_loop(0, rows // span, group, 0)


def scan_blocks(blocks, ends_ref, step_ref, modes, cols, start, out_ref=None):
    pitch = ends_ref.shape[0] // blocks
    groups = modes // 8
    steps = [step_ref[pl.ds(i * 8, 8), cols] for i in range(groups)]
    outs = [out_ref[pl.ds(i * 8, 8), cols] for i in range(groups)] if out_ref is not None else None
    states = list(start)
    for b in range(blocks):
        for i in range(groups):
            where = pl.ds(b * pitch + i * 8, 8)
            end = ends_ref[where, cols]
            if outs is not None:
                ends_ref[where, cols] = states[i] * outs[i]
            states[i] = states[i] * steps[i] + end
    return states


def respond(x_ref, hidden_ref, ends_ref, powers_ref, kernel_ref, result_ref, modes, cols):
    rows = x_ref.shape[0]
    blocks = rows // BLOCK
    span = 8 * BLOCK
    pitch = ends_ref.shape[0] // blocks

    def group(g, carry):
        base = pl.multiple_of(g * span, span)
        coefs = [ends_ref[pl.ds(g * 8 * pitch + n, 8, stride=pitch), cols] for n in range(modes)]
        xs = [x_ref[pl.ds(base + j, 8, stride=BLOCK), cols] for j in range(BLOCK)]
        for j in range(BLOCK):
            power = jnp.broadcast_to(powers_ref[pl.ds(j, 1), cols], (8, LANES))
            total = coefs[modes - 1]
            for n in range(modes - 2, -1, -1):
                total = total * power + coefs[n]
            total = total * power
            for i in range(j + 1):
                total = total + xs[i] * jnp.broadcast_to(
                    kernel_ref[pl.ds(j - i, 1), cols], (8, LANES)
                )
            where = pl.ds(base + j, 8, stride=BLOCK)
            gelu = 0.5 * total * (1.0 + lax.erf(total * 0.7071067811865476))
            result_ref[where, cols] = hidden_ref[where, cols] + gelu
        return carry

    lax.fori_loop(0, rows // span, group, 0)


MESH = pl.DeviceIdType.MESH


def decay_left(y):
    small = jnp.ones_like(y)
    for k in range(10, 1, -1):
        small = 1.0 - y * (1.0 / k) * small
    return jnp.where(y < 0.5, y * small, 1.0 - jnp.exp(-y))


def make_tables(l, cols, rows, step_ref, mix_ref, skip_ref, table_ref):
    modes = mix_ref.shape[1]
    step = step_ref[pl.ds(l, 1), cols]
    order = lax.broadcasted_iota(jnp.int32, (modes, LANES), 0).astype(jnp.float32) + 1.0
    rates = jnp.broadcast_to(step, (modes, LANES)) * order
    out = mix_ref[l, :, cols] * jnp.sqrt(decay_left(2.0 * rates))
    table_ref[l, pl.ds(0, modes), cols] = jnp.exp(-rates)
    table_ref[l, pl.ds(modes, modes), cols] = jnp.exp(-rates * BLOCK)
    table_ref[l, pl.ds(2 * modes, modes), cols] = jnp.exp(-rates * rows)
    table_ref[l, pl.ds(3 * modes, modes), cols] = out
    lags = lax.broadcasted_iota(jnp.int32, (BLOCK, LANES), 0).astype(jnp.float32) + 1.0
    table_ref[l, pl.ds(4 * modes, BLOCK), cols] = jnp.exp(-lags * jnp.broadcast_to(step, (BLOCK, LANES)))
    skip = skip_ref[pl.ds(l, 1), cols]
    for j in range(BLOCK):
        terms = out * jnp.exp(-float(j) * rates) if j else out
        line = jnp.sum(terms, axis=0, keepdims=True)
        table_ref[l, pl.ds(5 * modes + j, 1), cols] = line if j else line + skip


def section_kernel(
    highs, signal_ref, weight_ref, gain_in, step_in, mix_in, skip_in, out_ref,
    raw_ref, all_ref, cols_ref, first_ref, hidden_ref, x_ref, ends_ref, table_ref,
    gain_ref, step_ref, mix_ref, skip_ref, stats_ref, last_ref, states_ref, rounded_ref, sems
):
    part, place = lax.axis_index("parts"), lax.axis_index("tm")
    high, low = place // SPLIT, place % SPLIT
    depth, width = weight_ref.shape[0], cols_ref.shape[1]
    fine, channels = signal_ref.shape
    half = depth // 2
    cuts = 2 if half % 32 == 0 else 1
    cut = half // cuts
    own_rows = fine // POOL
    rows = own_rows * SPLIT
    piece = own_rows // PIECES
    chunk = SPLIT * depth
    groups = width // LANES
    layers, modes = mix_ref.shape[0], mix_ref.shape[1]
    blocks = rows // BLOCK
    last_step = highs - 1
    other = 1 - part
    exact = lax.Precision.HIGHEST
    (near_send, near_recv, own_sem, line_send, line_recv, side_send, side_recv, rows_send, rows_recv,
     stats_send, stats_recv, state_send, state_recv, out_send, out_recv) = sems
    flip = lambda bit: low + bit - 2 * bit * ((low // bit) % 2)
    core, cross, diagonal = flip(1), flip(2), SPLIT - 1 - low
    near_by = (core, cross, diagonal)
    queue = (low, core, cross, diagonal)
    at = lambda p, h, l: (p, h * SPLIT + l)
    own_cols = pl.ds(pl.multiple_of(low * width, width), width)

    own_copies = [
        pltpu.make_async_copy(signal_ref, raw_ref, own_sem.at[0]),
        pltpu.make_async_copy(
            weight_ref.at[:, own_cols],
            cols_ref.at[pl.ds(pl.multiple_of(high * chunk + low * depth, depth), depth), :],
            own_sem.at[1],
        ),
        pltpu.make_async_copy(gain_in.at[:, own_cols], gain_ref, own_sem.at[2]),
        pltpu.make_async_copy(step_in.at[:, own_cols], step_ref, own_sem.at[3]),
        pltpu.make_async_copy(mix_in.at[:, :, own_cols], mix_ref, own_sem.at[4]),
        pltpu.make_async_copy(skip_in.at[:, own_cols], skip_ref, own_sem.at[5]),
    ]
    for copy in own_copies:
        copy.start()

    barrier = pltpu.get_barrier_semaphore()

    def greet(device):
        pl.semaphore_signal(barrier, inc=1, device_id=device, device_id_type=MESH)

    for who in near_by:
        greet(at(part, high, who))
    greet(at(other, high, low))

    def greet_high(h, carry):
        pl.when(h != high)(lambda: greet(at(part, h, low)))
        return carry

    lax.fori_loop(0, highs, greet_high, 0)
    pl.semaphore_wait(barrier, 4 + highs - 1)

    def spot(h, l, which, c):
        start = pl.multiple_of(h * chunk + l * depth + which * half + c * cut, cut)
        return cols_ref.at[pl.ds(start, cut), :]

    def source(to, which, c):
        return weight_ref.at[
            pl.ds(pl.multiple_of(which * half + c * cut, cut), cut),
            pl.ds(pl.multiple_of(to * width, width), width),
        ]

    def near(bit, which, c):
        to = near_by[bit]
        return pltpu.make_async_remote_copy(
            source(to, which, c), spot(high, low, which, c), near_send.at[bit, which, c],
            near_recv.at[bit, which, c], device_id=at(part, high, to), device_id_type=MESH,
        )

    def near_arrived(bit, which, c):
        where = spot(high, near_by[bit], which, c)
        pltpu.make_async_remote_copy(
            where, where, near_send.at[bit, which, c], near_recv.at[bit, which, c],
            device_id=at(part, high, near_by[bit]), device_id_type=MESH,
        ).wait_recv()

    def line(up, h, l, c, own=False):
        to = jnp.clip(high + (1 if up else -1), 0, highs - 1)
        return pltpu.make_async_remote_copy(
            source(low, part, c) if own else spot(h, l, part, c), spot(h, l, part, c),
            line_send.at[int(up), h, l, c], line_recv.at[h, l, c],
            device_id=at(part, to, low), device_id_type=MESH,
        )

    def both_ways(l, c, own=False):
        pl.when(high < highs - 1)(lambda: line(True, high, l, c, own).start())
        pl.when(high > 0)(lambda: line(False, high, l, c, own).start())

    def side(h, l, which, c):
        return pltpu.make_async_remote_copy(
            spot(h, l, which, c), spot(h, l, which, c), side_send.at[h, l, c], side_recv.at[h, l, c],
            device_id=at(other, high, low), device_id_type=MESH,
        )

    def block(owner, p):
        start = pl.multiple_of(owner * own_rows + p * piece, piece)
        return all_ref.at[pl.ds(start, piece), :]

    def give(bit, p):
        return pltpu.make_async_remote_copy(
            block(low, p), block(low, p), rows_send.at[bit, p], rows_recv.at[bit, p],
            device_id=at(part, high, near_by[bit]), device_id_type=MESH,
        )

    def taken(bit, p):
        where = block(near_by[bit], p)
        pltpu.make_async_remote_copy(
            where, where, rows_send.at[bit, p], rows_recv.at[bit, p],
            device_id=at(part, high, core), device_id_type=MESH,
        ).wait_recv()

    def pass_on(p):
        return pltpu.make_async_remote_copy(
            block(cross, p), block(cross, p), rows_send.at[2, p], rows_recv.at[2, p],
            device_id=at(part, high, core), device_id_type=MESH,
        )

    for c in range(cuts):
        both_ways(low, c, True)
    for bit in (1, 2, 0):
        for c in range(cuts):
            near(bit, part, c).start()

    own_copies[0].wait()
    line_of = lax.broadcasted_iota(jnp.int32, (own_rows, fine), 0)
    tick = lax.broadcasted_iota(jnp.int32, (own_rows, fine), 1)
    own_start = pl.multiple_of(low * own_rows, own_rows)
    for q in range(POOL):
        pick = (tick == POOL * line_of + q).astype(jnp.bfloat16)
        picked = jnp.dot(pick, raw_ref[...], preferred_element_type=jnp.float32)
        all_ref[pl.ds(own_start, own_rows), pl.ds(q * channels, channels)] = picked.astype(jnp.bfloat16)

    for p in range(PIECES):
        give(1, p).start()
    for p in range(PIECES):
        give(0, p).start()
    for bit in (1, 2, 0):
        for c in range(cuts):
            near(bit, other, c).start()
    for c in range(cuts):
        near_arrived(0, part, c)
        both_ways(core, c)

    for copy in own_copies[1:]:
        copy.wait()

    def lanes(g):
        return pl.ds(pl.multiple_of(g * LANES, LANES), LANES)

    def tables_of(l):
        def one(g, carry):
            make_tables(l, lanes(g), rows, step_ref, mix_ref, skip_ref, table_ref)
            return carry

        lax.fori_loop(0, groups, one, 0)

    tables_of(0)

    def relay(s, l, c):
        @pl.when(high - s >= 0)
        def _():
            h = high - s
            line(True, h, l, c).wait_recv()
            pl.when(high < highs - 1)(lambda: line(True, h, l, c).start())
            side(h, l, part, c).start()

        @pl.when(high + s < highs)
        def _():
            h = high + s
            line(False, h, l, c).wait_recv()
            pl.when(high > 0)(lambda: line(False, h, l, c).start())
            side(h, l, part, c).start()

    def rows_on(p):
        taken(1, p)
        pass_on(p).start()

    for bit, l in ((1, low), (2, core)):
        for c in range(cuts):
            near_arrived(bit, part, c)
            both_ways(near_by[bit], c)
            relay(1, l, c)
    for layer in range(1, layers):
        tables_of(layer)
    for l in (cross, diagonal):
        for c in range(cuts):
            relay(1, l, c)
    rows_on(0)

    def step(s, carry):
        for l in (low, core):
            for c in range(cuts):
                relay(s, l, c)
        pl.when(s == 2)(lambda: rows_on(1))
        for l in (cross, diagonal):
            for c in range(cuts):
                relay(s, l, c)
        pl.when(s == 2)(lambda: rows_on(2))
        return carry

    lax.fori_loop(2, last_step, step, 0)

    def multiply(start, size):
        start = pl.multiple_of(start, size)
        return jnp.dot(
            all_ref[:, pl.ds(start, size)], cols_ref[pl.ds(start, size), :],
            preferred_element_type=jnp.float32,
        )

    def keep(value, fresh):
        for g in range(groups):
            piece_of = value[:, g * LANES : (g + 1) * LANES]
            first_ref[g] = piece_of if fresh else first_ref[g] + piece_of

    def side_arrived(h, l):
        for c in range(cuts):
            side(h, l, other, c).wait_recv()

    def add(s, carry):
        for h, there in ((high - s, high - s >= 0), (high + s, high + s < highs)):
            @pl.when(there)
            def _(h=h):
                for l in queue:
                    side_arrived(h, l)
                keep(multiply(h * chunk, chunk), False)

        return carry

    def add_each(s, carry):
        if depth % LANES:
            return add(s, carry)

        for h, there in ((high - s, high - s >= 0), (high + s, high + s < highs)):
            @pl.when(there)
            def _(h=h):
                for l in queue:
                    side_arrived(h, l)
                    keep(multiply(h * chunk + l * depth, depth), False)

        return carry

    for l in (low, core):
        for c in range(cuts):
            relay(last_step, l, c)
    rows_on(3)
    relay(last_step, cross, 0)
    first_ref[...] = jnp.zeros_like(first_ref)
    for p in range(PIECES):
        taken(0, p)
        taken(2, p)
    add(1, 0)
    for c in range(1, cuts):
        relay(last_step, cross, c)
    relay(last_step, diagonal, 0)
    for bit in range(3):
        for c in range(cuts):
            near_arrived(bit, other, c)
    keep(multiply(high * chunk, chunk), False)
    for c in range(1, cuts):
        relay(last_step, diagonal, c)
    lax.fori_loop(2, highs, add_each, 0)

    def stats_copy(l, bit, owner):
        return pltpu.make_async_remote_copy(
            stats_ref.at[l, owner], stats_ref.at[l, owner], stats_send.at[l, bit],
            stats_recv.at[l, bit], device_id=at(part, high, near_by[bit]), device_id_type=MESH,
        )

    def state_copy(l, g, origin, target):
        return pltpu.make_async_remote_copy(
            last_ref.at[l, g], states_ref.at[l, origin, g], state_send.at[l, target, g],
            state_recv.at[l, origin, g], device_id=at(part, target, low), device_id_type=MESH,
        )

    def out_cols(owner, g):
        return pl.ds(pl.multiple_of(owner * width + g * LANES, LANES), LANES)

    def out_copy(g, bit, owner):
        start = pl.multiple_of(near_by[bit] * own_rows, own_rows)
        return pltpu.make_async_remote_copy(
            rounded_ref.at[g, pl.ds(start, own_rows), :], out_ref.at[:, out_cols(owner, g)],
            out_send.at[g, bit], out_recv.at[g, bit],
            device_id=at(part, high, near_by[bit]), device_id_type=MESH,
        )

    def own_out(g):
        return pltpu.make_async_copy(
            rounded_ref.at[g, pl.ds(own_start, own_rows), :], out_ref.at[:, out_cols(low, g)], own_sem.at[6 + g]
        )

    for l in range(layers):
        source_ref = first_ref if l == 0 else hidden_ref
        total = source_ref[0]
        for g in range(1, groups):
            total = total + source_ref[g]
        mean = jnp.sum(total, axis=-1, keepdims=True) / width
        square = jnp.square(source_ref[0] - mean)
        for g in range(1, groups):
            square = square + jnp.square(source_ref[g] - mean)
        ones = jnp.ones((8, LANES), jnp.float32)
        across = lambda v: lax.dot_general(
            ones, v, (((1,), (1,)), ((), ())), precision=exact, preferred_element_type=jnp.float32
        )
        row_of = lax.broadcasted_iota(jnp.int32, (8, rows), 0)
        stats_ref[l, low] = jnp.where(row_of == 0, across(total) / width, across(square))
        for bit in (1, 2, 0):
            stats_copy(l, bit, low).start()
        for bit in range(3):
            stats_copy(l, bit, near_by[bit]).wait_recv()
        every = [stats_ref[l, i] for i in range(SPLIT)]
        means = [e[0:1] for e in every]
        row_mean = (means[0] + means[1] + means[2] + means[3]) / SPLIT
        row_var = sum(e[1:2] + width * jnp.square(e[0:1] - row_mean) for e in every)
        row_scale = lax.rsqrt(row_var / (width * SPLIT) + 1e-05)
        both = jnp.transpose(jnp.where(row_of == 0, row_mean, row_scale))
        row_mean, row_scale = both[:, 0:1], both[:, 1:2]
        for g in range(groups):
            gain = gain_ref[pl.ds(l, 1), pl.ds(g * LANES, LANES)]
            x_ref[g] = (source_ref[g] - row_mean) * row_scale * gain

        def table(index, g, size):
            return table_ref.at[l, pl.ds(index * modes, size), lanes(g)]

        cols = slice(None)
        eights = modes // 8

        def send(g):
            def one(h, carry):
                pl.when(h > high)(lambda: state_copy(l, g, high, h).start())
                return carry

            lax.fori_loop(1, highs, one, 0)

        def ends(g, carry):
            block_ends(x_ref.at[g], table(0, g, modes), ends_ref.at[g], modes, cols)
            zero = [jnp.zeros((8, LANES), jnp.float32)] * eights
            last = scan_blocks(blocks, ends_ref.at[g], table(1, g, modes), modes, cols, zero)
            for i in range(eights):
                last_ref[l, g, pl.ds(i * 8, 8), :] = last[i]
            send(g)
            return carry

        lax.fori_loop(0, groups, ends, 0)

        def finish(g, carry):
            whole = table(2, g, modes)

            def join(h, start):
                @pl.when(h < high)
                def _():
                    state_copy(l, g, h, high).wait_recv()
                    states_ref[l, high, g] = whole[...] * states_ref[l, high, g] + states_ref[l, h, g]
                return start

            states_ref[l, high, g] = jnp.zeros((modes, LANES), jnp.float32)
            lax.fori_loop(0, highs - 1, join, 0)
            start = [states_ref[l, high, g, pl.ds(i * 8, 8), :] for i in range(eights)]
            scan_blocks(
                blocks, ends_ref.at[g], table(1, g, modes), modes, cols, start, table(3, g, modes)
            )
            respond(
                x_ref.at[g], source_ref.at[g], ends_ref.at[g], table(4, g, BLOCK),
                table(5, g, BLOCK), hidden_ref.at[g], modes, cols,
            )
            if l == layers - 1:
                rounded_ref[g] = hidden_ref[g].astype(jnp.bfloat16)
                for bit in (1, 2, 0):
                    out_copy(g, bit, low).start()
                own_out(g).start()
            return carry

        lax.fori_loop(0, groups, finish, 0)

    def drain(g, carry):
        own_out(g).wait()
        for bit in range(3):
            out_copy(g, bit, near_by[bit]).wait_recv()
            out_copy(g, bit, low).wait_send()

        def one(h, carry):
            @pl.when(h > high)
            def _():
                for l in range(layers):
                    state_copy(l, g, high, h).wait_send()
            return carry

        return lax.fori_loop(1, highs, one, carry)

    for bit in range(3):
        for c in range(cuts):
            near(bit, 0, c).wait_send()
            near(bit, 1, c).wait_send()
    for p in range(PIECES):
        give(0, p).wait_send()
        give(1, p).wait_send()
        pass_on(p).wait_send()

    def sent(h, carry):
        for l in range(SPLIT):
            for c in range(cuts):
                pl.when((h <= high) & (high < highs - 1))(lambda: line(True, h, l, c).wait_send())
                pl.when((h >= high) & (high > 0))(lambda: line(False, h, l, c).wait_send())
                pl.when(h != high)(lambda: side(h, l, part, c).wait_send())
        return carry

    lax.fori_loop(0, highs, sent, 0)
    for l in range(layers):
        for bit in range(3):
            stats_copy(l, bit, low).wait_send()
    lax.fori_loop(0, groups, drain, 0)


def local(signal, pool_weight, norm_gain, step_size, mode_out, skip_gain):
    fine, channels = signal.shape
    depth, total = pool_weight.shape
    layers, modes, _ = mode_out.shape
    own_rows = fine // POOL
    rows = own_rows * SPLIT
    width = total // SPLIT
    groups = width // LANES
    highs = lax.axis_size("tm") // SPLIT
    cuts = 2 if depth % 64 == 0 else 1
    dma = pltpu.SemaphoreType.DMA
    vmem, f32, b16 = pltpu.VMEM, jnp.float32, jnp.bfloat16
    anywhere = pl.BlockSpec(memory_space=pl.ANY)
    return pl.pallas_call(
        functools.partial(section_kernel, highs),
        out_shape=jax.ShapeDtypeStruct((own_rows, total), b16),
        in_specs=[anywhere] * 6,
        out_specs=anywhere,
        scratch_shapes=[
            vmem((fine, channels), b16),
            vmem((rows, POOL * channels), b16),
            vmem((POOL * channels, width), b16),
            vmem((groups, rows, LANES), f32),
            vmem((groups, rows, LANES), f32),
            vmem((groups, rows, LANES), f32),
            vmem((groups, (modes + PAD) * (rows // BLOCK), LANES), f32),
            vmem((layers, 6 * modes, width), f32),
            vmem((layers, width), f32),
            vmem((layers, width), f32),
            vmem((layers, modes, width), f32),
            vmem((layers, width), f32),
            vmem((layers, SPLIT, 8, rows), f32),
            vmem((layers, groups, modes, LANES), f32),
            vmem((layers, highs, groups, modes, LANES), f32),
            vmem((groups, rows, LANES), b16),
            [
                dma((3, 2, cuts)), dma((3, 2, cuts)), dma((6 + groups,)),
                dma((2, highs, SPLIT, cuts)), dma((highs, SPLIT, cuts)),
                dma((highs, SPLIT, cuts)), dma((highs, SPLIT, cuts)),
                dma((3, PIECES)), dma((3, PIECES)),
                dma((layers, 3)), dma((layers, 3)), dma((layers, highs, groups)),
                dma((layers, highs, groups)), dma((groups, 3)), dma((groups, 3)),
            ],
        ],
        compiler_params=pltpu.CompilerParams(
            collective_id=0, has_side_effects=True, vmem_limit_bytes=48 << 20
        ),
    )(signal, pool_weight, norm_gain, step_size, mode_out, skip_gain)


def solution(mesh):
    placed = (P(("parts", "tm"), None), P("tm", None), P(), P(), P(), P())
    return jax.shard_map(
        local, mesh=mesh, in_specs=placed, out_specs=P(("parts", "tm"), None), check_vma=False
    )
```

```python
import functools

import jax
import jax.numpy as jnp
from jax import lax
from jax.experimental import pallas as pl
from jax.experimental.pallas import tpu as pltpu
from jax.sharding import PartitionSpec as P

POOL = 4
SPLIT = 4
BLOCK = 16
LANES = 128
PIECES = 4
PAD = 1


def block_ends(x_ref, decay_ref, ends_ref, modes, cols):
    rows = x_ref.shape[0]
    blocks = rows // BLOCK
    span = 8 * BLOCK
    pitch = ends_ref.shape[0] // blocks

    def group(g, carry):
        base = pl.multiple_of(g * span, span)
        xs = [x_ref[pl.ds(base + j, 8, stride=BLOCK), cols] for j in range(BLOCK)]
        for n in range(modes):
            decay = jnp.broadcast_to(decay_ref[pl.ds(n, 1), cols], (8, LANES))
            end = xs[0]
            for j in range(1, BLOCK):
                end = end * decay + xs[j]
            ends_ref[pl.ds(g * 8 * pitch + n, 8, stride=pitch), cols] = end
        return carry

    lax.fori_loop(0, rows // span, group, 0)


def scan_blocks(blocks, ends_ref, step_ref, modes, cols, start, out_ref=None):
    pitch = ends_ref.shape[0] // blocks
    groups = modes // 8
    steps = [step_ref[pl.ds(i * 8, 8), cols] for i in range(groups)]
    outs = [out_ref[pl.ds(i * 8, 8), cols] for i in range(groups)] if out_ref is not None else None
    states = list(start)
    for b in range(blocks):
        for i in range(groups):
            where = pl.ds(b * pitch + i * 8, 8)
            end = ends_ref[where, cols]
            if outs is not None:
                ends_ref[where, cols] = states[i] * outs[i]
            states[i] = states[i] * steps[i] + end
    return states


def respond(x_ref, hidden_ref, ends_ref, powers_ref, kernel_ref, result_ref, modes, cols):
    rows = x_ref.shape[0]
    blocks = rows // BLOCK
    span = 8 * BLOCK
    pitch = ends_ref.shape[0] // blocks

    def group(g, carry):
        base = pl.multiple_of(g * span, span)
        coefs = [ends_ref[pl.ds(g * 8 * pitch + n, 8, stride=pitch), cols] for n in range(modes)]
        xs = [x_ref[pl.ds(base + j, 8, stride=BLOCK), cols] for j in range(BLOCK)]
        for j in range(BLOCK):
            power = jnp.broadcast_to(powers_ref[pl.ds(j, 1), cols], (8, LANES))
            total = coefs[modes - 1]
            for n in range(modes - 2, -1, -1):
                total = total * power + coefs[n]
            total = total * power
            for i in range(j + 1):
                total = total + xs[i] * jnp.broadcast_to(
                    kernel_ref[pl.ds(j - i, 1), cols], (8, LANES)
                )
            where = pl.ds(base + j, 8, stride=BLOCK)
            gelu = 0.5 * total * (1.0 + lax.erf(total * 0.7071067811865476))
            result_ref[where, cols] = hidden_ref[where, cols] + gelu
        return carry

    lax.fori_loop(0, rows // span, group, 0)


MESH = pl.DeviceIdType.MESH


def decay_left(y):
    small = jnp.ones_like(y)
    for k in range(10, 1, -1):
        small = 1.0 - y * (1.0 / k) * small
    return jnp.where(y < 0.5, y * small, 1.0 - jnp.exp(-y))


def make_tables(l, cols, rows, step_ref, mix_ref, skip_ref, table_ref):
    modes = mix_ref.shape[1]
    step = step_ref[pl.ds(l, 1), cols]
    order = lax.broadcasted_iota(jnp.int32, (modes, LANES), 0).astype(jnp.float32) + 1.0
    rates = jnp.broadcast_to(step, (modes, LANES)) * order
    out = mix_ref[l, :, cols] * jnp.sqrt(decay_left(2.0 * rates))
    table_ref[l, pl.ds(0, modes), cols] = jnp.exp(-rates)
    table_ref[l, pl.ds(modes, modes), cols] = jnp.exp(-rates * BLOCK)
    table_ref[l, pl.ds(2 * modes, modes), cols] = jnp.exp(-rates * rows)
    table_ref[l, pl.ds(3 * modes, modes), cols] = out
    lags = lax.broadcasted_iota(jnp.int32, (BLOCK, LANES), 0).astype(jnp.float32) + 1.0
    table_ref[l, pl.ds(4 * modes, BLOCK), cols] = jnp.exp(-lags * jnp.broadcast_to(step, (BLOCK, LANES)))
    skip = skip_ref[pl.ds(l, 1), cols]
    for j in range(BLOCK):
        terms = out * jnp.exp(-float(j) * rates) if j else out
        line = jnp.sum(terms, axis=0, keepdims=True)
        table_ref[l, pl.ds(5 * modes + j, 1), cols] = line if j else line + skip


def section_kernel(
    highs, signal_ref, weight_ref, gain_in, step_in, mix_in, skip_in, out_ref,
    raw_ref, all_ref, cols_ref, first_ref, hidden_ref, x_ref, ends_ref, table_ref,
    gain_ref, step_ref, mix_ref, skip_ref, stats_ref, last_ref, states_ref, rounded_ref, sems
):
    part, place = lax.axis_index("parts"), lax.axis_index("tm")
    high, low = place // SPLIT, place % SPLIT
    depth, width = weight_ref.shape[0], cols_ref.shape[1]
    fine, channels = signal_ref.shape
    half = depth // 2
    cuts = 2 if half % 32 == 0 else 1
    cut = half // cuts
    own_rows = fine // POOL
    rows = own_rows * SPLIT
    piece = own_rows // PIECES
    chunk = SPLIT * depth
    groups = width // LANES
    layers, modes = mix_ref.shape[0], mix_ref.shape[1]
    blocks = rows // BLOCK
    last_step = highs - 1
    other = 1 - part
    exact = lax.Precision.HIGHEST
    (near_send, near_recv, own_sem, line_send, line_recv, side_send, side_recv, rows_send, rows_recv,
     stats_send, stats_recv, state_send, state_recv, out_send, out_recv) = sems
    flip = lambda bit: low + bit - 2 * bit * ((low // bit) % 2)
    core, cross, diagonal = flip(1), flip(2), SPLIT - 1 - low
    near_by = (core, cross, diagonal)
    queue = (low, core, cross, diagonal)
    at = lambda p, h, l: (p, h * SPLIT + l)
    own_cols = pl.ds(pl.multiple_of(low * width, width), width)

    own_copies = [
        pltpu.make_async_copy(signal_ref, raw_ref, own_sem.at[0]),
        pltpu.make_async_copy(
            weight_ref.at[:, own_cols],
            cols_ref.at[pl.ds(pl.multiple_of(high * chunk + low * depth, depth), depth), :],
            own_sem.at[1],
        ),
        pltpu.make_async_copy(gain_in.at[:, own_cols], gain_ref, own_sem.at[2]),
        pltpu.make_async_copy(step_in.at[:, own_cols], step_ref, own_sem.at[3]),
        pltpu.make_async_copy(mix_in.at[:, :, own_cols], mix_ref, own_sem.at[4]),
        pltpu.make_async_copy(skip_in.at[:, own_cols], skip_ref, own_sem.at[5]),
    ]
    for copy in own_copies:
        copy.start()

    barrier = pltpu.get_barrier_semaphore()

    def greet(device):
        pl.semaphore_signal(barrier, inc=1, device_id=device, device_id_type=MESH)

    for who in near_by:
        greet(at(part, high, who))
    greet(at(other, high, low))

    def greet_high(h, carry):
        pl.when(h != high)(lambda: greet(at(part, h, low)))
        return carry

    pl.when(high > 0)(lambda: greet(at(part, high - 1, low)))
    pl.when(high < highs - 1)(lambda: greet(at(part, high + 1, low)))
    pl.semaphore_wait(barrier, 4 + jnp.minimum(high, 1) + jnp.minimum(highs - 1 - high, 1))

    def spot(h, l, which, c):
        start = pl.multiple_of(h * chunk + l * depth + which * half + c * cut, cut)
        return cols_ref.at[pl.ds(start, cut), :]

    def source(to, which, c):
        return weight_ref.at[
            pl.ds(pl.multiple_of(which * half + c * cut, cut), cut),
            pl.ds(pl.multiple_of(to * width, width), width),
        ]

    def near(bit, which, c):
        to = near_by[bit]
        return pltpu.make_async_remote_copy(
            source(to, which, c), spot(high, low, which, c), near_send.at[bit, which, c],
            near_recv.at[bit, which, c], device_id=at(part, high, to), device_id_type=MESH,
        )

    def near_arrived(bit, which, c):
        where = spot(high, near_by[bit], which, c)
        pltpu.make_async_remote_copy(
            where, where, near_send.at[bit, which, c], near_recv.at[bit, which, c],
            device_id=at(part, high, near_by[bit]), device_id_type=MESH,
        ).wait_recv()

    def line(up, h, l, c, own=False):
        to = jnp.clip(high + (1 if up else -1), 0, highs - 1)
        return pltpu.make_async_remote_copy(
            source(low, part, c) if own else spot(h, l, part, c), spot(h, l, part, c),
            line_send.at[int(up), h, l, c], line_recv.at[h, l, c],
            device_id=at(part, to, low), device_id_type=MESH,
        )

    def both_ways(l, c, own=False):
        pl.when(high < highs - 1)(lambda: line(True, high, l, c, own).start())
        pl.when(high > 0)(lambda: line(False, high, l, c, own).start())

    def side(h, l, which, c):
        return pltpu.make_async_remote_copy(
            spot(h, l, which, c), spot(h, l, which, c), side_send.at[h, l, c], side_recv.at[h, l, c],
            device_id=at(other, high, low), device_id_type=MESH,
        )

    def block(owner, p):
        start = pl.multiple_of(owner * own_rows + p * piece, piece)
        return all_ref.at[pl.ds(start, piece), :]

    def give(bit, p):
        return pltpu.make_async_remote_copy(
            block(low, p), block(low, p), rows_send.at[bit, p], rows_recv.at[bit, p],
            device_id=at(part, high, near_by[bit]), device_id_type=MESH,
        )

    def taken(bit, p):
        where = block(near_by[bit], p)
        pltpu.make_async_remote_copy(
            where, where, rows_send.at[bit, p], rows_recv.at[bit, p],
            device_id=at(part, high, core), device_id_type=MESH,
        ).wait_recv()

    def pass_on(p):
        return pltpu.make_async_remote_copy(
            block(cross, p), block(cross, p), rows_send.at[2, p], rows_recv.at[2, p],
            device_id=at(part, high, core), device_id_type=MESH,
        )

    for c in range(cuts):
        both_ways(low, c, True)
    for bit in (1, 2, 0):
        for c in range(cuts):
            near(bit, part, c).start()

    own_copies[0].wait()
    line_of = lax.broadcasted_iota(jnp.int32, (own_rows, fine), 0)
    tick = lax.broadcasted_iota(jnp.int32, (own_rows, fine), 1)
    own_start = pl.multiple_of(low * own_rows, own_rows)
    for q in range(POOL):
        pick = (tick == POOL * line_of + q).astype(jnp.bfloat16)
        picked = jnp.dot(pick, raw_ref[...], preferred_element_type=jnp.float32)
        all_ref[pl.ds(own_start, own_rows), pl.ds(q * channels, channels)] = picked.astype(jnp.bfloat16)

    for p in range(PIECES):
        give(1, p).start()
    for p in range(PIECES):
        give(0, p).start()
    for bit in (1, 2, 0):
        for c in range(cuts):
            near(bit, other, c).start()
    for c in range(cuts):
        near_arrived(0, part, c)
        both_ways(core, c)

    for copy in own_copies[1:]:
        copy.wait()

    def lanes(g):
        return pl.ds(pl.multiple_of(g * LANES, LANES), LANES)

    def tables_of(l):
        def one(g, carry):
            make_tables(l, lanes(g), rows, step_ref, mix_ref, skip_ref, table_ref)
            return carry

        lax.fori_loop(0, groups, one, 0)

    tables_of(0)

    def relay(s, l, c):
        @pl.when(high - s >= 0)
        def _():
            h = high - s
            line(True, h, l, c).wait_recv()
            pl.when(high < highs - 1)(lambda: line(True, h, l, c).start())
            side(h, l, part, c).start()

        @pl.when(high + s < highs)
        def _():
            h = high + s
            line(False, h, l, c).wait_recv()
            pl.when(high > 0)(lambda: line(False, h, l, c).start())
            side(h, l, part, c).start()

    def rows_on(p):
        taken(1, p)
        pass_on(p).start()

    for bit, l in ((1, low), (2, core)):
        for c in range(cuts):
            near_arrived(bit, part, c)
            both_ways(near_by[bit], c)
            relay(1, l, c)
    for layer in range(1, layers):
        tables_of(layer)
    for l in (cross, diagonal):
        for c in range(cuts):
            relay(1, l, c)
    rows_on(0)

    def step(s, carry):
        for l in (low, core):
            for c in range(cuts):
                relay(s, l, c)
        pl.when(s == 2)(lambda: rows_on(1))
        for l in (cross, diagonal):
            for c in range(cuts):
                relay(s, l, c)
        pl.when(s == 2)(lambda: rows_on(2))
        return carry

    lax.fori_loop(2, last_step, step, 0)

    def multiply(start, size):
        start = pl.multiple_of(start, size)
        return jnp.dot(
            all_ref[:, pl.ds(start, size)], cols_ref[pl.ds(start, size), :],
            preferred_element_type=jnp.float32,
        )

    def keep(value, fresh):
        for g in range(groups):
            piece_of = value[:, g * LANES : (g + 1) * LANES]
            first_ref[g] = piece_of if fresh else first_ref[g] + piece_of

    def side_arrived(h, l):
        for c in range(cuts):
            side(h, l, other, c).wait_recv()

    def add(s, carry):
        for h, there in ((high - s, high - s >= 0), (high + s, high + s < highs)):
            @pl.when(there)
            def _(h=h):
                for l in queue:
                    side_arrived(h, l)
                keep(multiply(h * chunk, chunk), False)

        return carry

    def add_each(s, carry):
        if depth % LANES:
            return add(s, carry)

        for h, there in ((high - s, high - s >= 0), (high + s, high + s < highs)):
            @pl.when(there)
            def _(h=h):
                for l in queue:
                    side_arrived(h, l)
                    keep(multiply(h * chunk + l * depth, depth), False)

        return carry

    for l in (low, core):
        for c in range(cuts):
            relay(last_step, l, c)
    rows_on(3)
    relay(last_step, cross, 0)
    first_ref[...] = jnp.zeros_like(first_ref)
    for p in range(PIECES):
        taken(0, p)
        taken(2, p)
    add(1, 0)
    for c in range(1, cuts):
        relay(last_step, cross, c)
    relay(last_step, diagonal, 0)
    for bit in range(3):
        for c in range(cuts):
            near_arrived(bit, other, c)
    keep(multiply(high * chunk, chunk), False)
    for c in range(1, cuts):
        relay(last_step, diagonal, c)
    lax.fori_loop(2, highs, add_each, 0)

    def pool_sent():
        for bit in range(3):
            for c in range(cuts):
                near(bit, 0, c).wait_send()
                near(bit, 1, c).wait_send()
        for p in range(PIECES):
            give(0, p).wait_send()
            give(1, p).wait_send()
            pass_on(p).wait_send()

        def sent(h, carry):
            for l in range(SPLIT):
                for c in range(cuts):
                    pl.when((h <= high) & (high < highs - 1))(lambda: line(True, h, l, c).wait_send())
                    pl.when((h >= high) & (high > 0))(lambda: line(False, h, l, c).wait_send())
                    pl.when(h != high)(lambda: side(h, l, part, c).wait_send())
            return carry

        lax.fori_loop(0, highs, sent, 0)

    def stats_copy(l, bit, owner):
        return pltpu.make_async_remote_copy(
            stats_ref.at[l, owner], stats_ref.at[l, owner], stats_send.at[l, bit],
            stats_recv.at[l, bit], device_id=at(part, high, near_by[bit]), device_id_type=MESH,
        )

    def state_copy(l, g, origin, target):
        return pltpu.make_async_remote_copy(
            last_ref.at[l, g], states_ref.at[l, origin, g], state_send.at[l, target, g],
            state_recv.at[l, origin, g], device_id=at(part, target, low), device_id_type=MESH,
        )

    def out_cols(owner, g):
        return pl.ds(pl.multiple_of(owner * width + g * LANES, LANES), LANES)

    def out_copy(g, bit, owner):
        start = pl.multiple_of(near_by[bit] * own_rows, own_rows)
        return pltpu.make_async_remote_copy(
            rounded_ref.at[g, pl.ds(start, own_rows), :], out_ref.at[:, out_cols(owner, g)],
            out_send.at[g, bit], out_recv.at[g, bit],
            device_id=at(part, high, near_by[bit]), device_id_type=MESH,
        )

    def own_out(g):
        return pltpu.make_async_copy(
            rounded_ref.at[g, pl.ds(own_start, own_rows), :], out_ref.at[:, out_cols(low, g)], own_sem.at[6 + g]
        )

    for l in range(layers):
        source_ref = first_ref if l == 0 else hidden_ref
        total = source_ref[0]
        for g in range(1, groups):
            total = total + source_ref[g]
        mean = jnp.sum(total, axis=-1, keepdims=True) / width
        square = jnp.square(source_ref[0] - mean)
        for g in range(1, groups):
            square = square + jnp.square(source_ref[g] - mean)
        ones = jnp.ones((8, LANES), jnp.float32)
        across = lambda v: lax.dot_general(
            ones, v, (((1,), (1,)), ((), ())), precision=exact, preferred_element_type=jnp.float32
        )
        row_of = lax.broadcasted_iota(jnp.int32, (8, rows), 0)
        stats_ref[l, low] = jnp.where(row_of == 0, across(total) / width, across(square))
        for bit in (1, 2, 0):
            stats_copy(l, bit, low).start()
        if l == 0:
            pool_sent()
        for bit in range(3):
            stats_copy(l, bit, near_by[bit]).wait_recv()
        every = [stats_ref[l, i] for i in range(SPLIT)]
        means = [e[0:1] for e in every]
        row_mean = (means[0] + means[1] + means[2] + means[3]) / SPLIT
        row_var = sum(e[1:2] + width * jnp.square(e[0:1] - row_mean) for e in every)
        row_scale = lax.rsqrt(row_var / (width * SPLIT) + 1e-05)
        both = jnp.transpose(jnp.where(row_of == 0, row_mean, row_scale))
        row_mean, row_scale = both[:, 0:1], both[:, 1:2]
        for g in range(groups):
            gain = gain_ref[pl.ds(l, 1), pl.ds(g * LANES, LANES)]
            x_ref[g] = (source_ref[g] - row_mean) * row_scale * gain

        def table(index, g, size):
            return table_ref.at[l, pl.ds(index * modes, size), lanes(g)]

        cols = slice(None)
        eights = modes // 8

        def send(g):
            def one(h, carry):
                pl.when(h > high)(lambda: state_copy(l, g, high, h).start())
                return carry

            lax.fori_loop(1, highs, one, 0)

        def ends(g, carry):
            block_ends(x_ref.at[g], table(0, g, modes), ends_ref.at[g], modes, cols)
            zero = [jnp.zeros((8, LANES), jnp.float32)] * eights
            last = scan_blocks(blocks, ends_ref.at[g], table(1, g, modes), modes, cols, zero)
            for i in range(eights):
                last_ref[l, g, pl.ds(i * 8, 8), :] = last[i]
            send(g)
            return carry

        lax.fori_loop(0, groups, ends, 0)

        def finish(g, carry):
            whole = table(2, g, modes)

            def join(h, start):
                @pl.when(h < high)
                def _():
                    state_copy(l, g, h, high).wait_recv()
                    states_ref[l, high, g] = whole[...] * states_ref[l, high, g] + states_ref[l, h, g]
                return start

            states_ref[l, high, g] = jnp.zeros((modes, LANES), jnp.float32)
            lax.fori_loop(0, highs - 1, join, 0)
            start = [states_ref[l, high, g, pl.ds(i * 8, 8), :] for i in range(eights)]
            scan_blocks(
                blocks, ends_ref.at[g], table(1, g, modes), modes, cols, start, table(3, g, modes)
            )
            respond(
                x_ref.at[g], source_ref.at[g], ends_ref.at[g], table(4, g, BLOCK),
                table(5, g, BLOCK), hidden_ref.at[g], modes, cols,
            )
            if l == layers - 1:
                rounded_ref[g] = hidden_ref[g].astype(jnp.bfloat16)
                for bit in (1, 2, 0):
                    out_copy(g, bit, low).start()
                own_out(g).start()
            return carry

        lax.fori_loop(0, groups, finish, 0)

    def drain(g, carry):
        own_out(g).wait()
        for bit in range(3):
            out_copy(g, bit, near_by[bit]).wait_recv()
            out_copy(g, bit, low).wait_send()

        def one(h, carry):
            @pl.when(h > high)
            def _():
                for l in range(layers):
                    state_copy(l, g, high, h).wait_send()
            return carry

        return lax.fori_loop(1, highs, one, carry)

    for l in range(layers):
        for bit in range(3):
            stats_copy(l, bit, low).wait_send()
    lax.fori_loop(0, groups, drain, 0)


def local(signal, pool_weight, norm_gain, step_size, mode_out, skip_gain):
    fine, channels = signal.shape
    depth, total = pool_weight.shape
    layers, modes, _ = mode_out.shape
    own_rows = fine // POOL
    rows = own_rows * SPLIT
    width = total // SPLIT
    groups = width // LANES
    highs = lax.axis_size("tm") // SPLIT
    cuts = 2 if depth % 64 == 0 else 1
    dma = pltpu.SemaphoreType.DMA
    vmem, f32, b16 = pltpu.VMEM, jnp.float32, jnp.bfloat16
    anywhere = pl.BlockSpec(memory_space=pl.ANY)
    far = pl.BlockSpec(memory_space=pltpu.HBM)
    return pl.pallas_call(
        functools.partial(section_kernel, highs),
        out_shape=jax.ShapeDtypeStruct((own_rows, total), b16),
        in_specs=[far] * 6,
        out_specs=anywhere,
        scratch_shapes=[
            vmem((fine, channels), b16),
            vmem((rows, POOL * channels), b16),
            vmem((POOL * channels, width), b16),
            vmem((groups, rows, LANES), f32),
            vmem((groups, rows, LANES), f32),
            vmem((groups, rows, LANES), f32),
            vmem((groups, (modes + PAD) * (rows // BLOCK), LANES), f32),
            vmem((layers, 6 * modes, width), f32),
            vmem((layers, width), f32),
            vmem((layers, width), f32),
            vmem((layers, modes, width), f32),
            vmem((layers, width), f32),
            vmem((layers, SPLIT, 8, rows), f32),
            vmem((layers, groups, modes, LANES), f32),
            vmem((layers, highs, groups, modes, LANES), f32),
            vmem((groups, rows, LANES), b16),
            [
                dma((3, 2, cuts)), dma((3, 2, cuts)), dma((6 + groups,)),
                dma((2, highs, SPLIT, cuts)), dma((highs, SPLIT, cuts)),
                dma((highs, SPLIT, cuts)), dma((highs, SPLIT, cuts)),
                dma((3, PIECES)), dma((3, PIECES)),
                dma((layers, 3)), dma((layers, 3)), dma((layers, highs, groups)),
                dma((layers, highs, groups)), dma((groups, 3)), dma((groups, 3)),
            ],
        ],
        compiler_params=pltpu.CompilerParams(
            collective_id=0, has_side_effects=True, vmem_limit_bytes=57000000
        ),
    )(signal, pool_weight, norm_gain, step_size, mode_out, skip_gain)


def solution(mesh):
    placed = (P(("parts", "tm"), None), P("tm", None), P(), P(), P(), P())
    return jax.shard_map(
        local, mesh=mesh, in_specs=placed, out_specs=P(("parts", "tm"), None), check_vma=False
    )
```

```python
import functools

import jax
import jax.numpy as jnp
from jax import lax
from jax.experimental import pallas as pl
from jax.experimental.pallas import tpu as pltpu
from jax.sharding import PartitionSpec as P

POOL = 4
SPLIT = 4
BLOCK = 16
LANES = 128
PIECES = 4
PAD = 1


def block_ends(x_ref, decay_ref, ends_ref, modes, cols, first, count):
    blocks = x_ref.shape[0] // BLOCK
    span = 8 * BLOCK
    pitch = ends_ref.shape[0] // blocks

    def group(g, carry):
        base = pl.multiple_of(g * span, span)
        xs = [x_ref[pl.ds(base + j, 8, stride=BLOCK), cols] for j in range(BLOCK)]
        for n in range(modes):
            decay = jnp.broadcast_to(decay_ref[pl.ds(n, 1), cols], (8, LANES))
            end = xs[0]
            for j in range(1, BLOCK):
                end = end * decay + xs[j]
            ends_ref[pl.ds(g * 8 * pitch + n, 8, stride=pitch), cols] = end
        return carry

    lax.fori_loop(first, first + count, group, 0)


def scan_blocks(blocks, ends_ref, step_ref, modes, cols, start, out_ref=None):
    pitch = ends_ref.shape[0] // blocks
    groups = modes // 8
    steps = [step_ref[pl.ds(i * 8, 8), cols] for i in range(groups)]
    outs = [out_ref[pl.ds(i * 8, 8), cols] for i in range(groups)] if out_ref is not None else None
    states = list(start)
    for b in range(blocks):
        for i in range(groups):
            where = pl.ds(b * pitch + i * 8, 8)
            end = ends_ref[where, cols]
            if outs is not None:
                ends_ref[where, cols] = states[i] * outs[i]
            states[i] = states[i] * steps[i] + end
    return states


def respond(
    x_ref, hidden_ref, ends_ref, powers_ref, kernel_ref, result_ref, modes, cols, first, count
):
    blocks = x_ref.shape[0] // BLOCK
    span = 8 * BLOCK
    pitch = ends_ref.shape[0] // blocks

    def group(g, carry):
        base = pl.multiple_of(g * span, span)
        coefs = [ends_ref[pl.ds(g * 8 * pitch + n, 8, stride=pitch), cols] for n in range(modes)]
        xs = [x_ref[pl.ds(base + j, 8, stride=BLOCK), cols] for j in range(BLOCK)]
        for j in range(BLOCK):
            power = jnp.broadcast_to(powers_ref[pl.ds(j, 1), cols], (8, LANES))
            total = coefs[modes - 1]
            for n in range(modes - 2, -1, -1):
                total = total * power + coefs[n]
            total = total * power
            for i in range(j + 1):
                total = total + xs[i] * jnp.broadcast_to(
                    kernel_ref[pl.ds(j - i, 1), cols], (8, LANES)
                )
            where = pl.ds(base + j, 8, stride=BLOCK)
            gelu = 0.5 * total * (1.0 + lax.erf(total * 0.7071067811865476))
            result_ref[where, cols] = hidden_ref[where, cols] + gelu
        return carry

    lax.fori_loop(first, first + count, group, 0)


MESH = pl.DeviceIdType.MESH


def decay_left(y):
    small = jnp.ones_like(y)
    for k in range(10, 1, -1):
        small = 1.0 - y * (1.0 / k) * small
    return jnp.where(y < 0.5, y * small, 1.0 - jnp.exp(-y))


def make_tables(l, cols, rows, step_ref, mix_ref, skip_ref, table_ref):
    modes = mix_ref.shape[1]
    step = step_ref[pl.ds(l, 1), cols]
    order = lax.broadcasted_iota(jnp.int32, (modes, LANES), 0).astype(jnp.float32) + 1.0
    rates = jnp.broadcast_to(step, (modes, LANES)) * order
    out = mix_ref[l, :, cols] * jnp.sqrt(decay_left(2.0 * rates))
    table_ref[l, pl.ds(0, modes), cols] = jnp.exp(-rates)
    table_ref[l, pl.ds(modes, modes), cols] = jnp.exp(-rates * BLOCK)
    table_ref[l, pl.ds(2 * modes, modes), cols] = jnp.exp(-rates * rows)
    table_ref[l, pl.ds(3 * modes, modes), cols] = out
    lags = lax.broadcasted_iota(jnp.int32, (BLOCK, LANES), 0).astype(jnp.float32) + 1.0
    table_ref[l, pl.ds(4 * modes, BLOCK), cols] = jnp.exp(-lags * jnp.broadcast_to(step, (BLOCK, LANES)))
    skip = skip_ref[pl.ds(l, 1), cols]
    for j in range(BLOCK):
        terms = out * jnp.exp(-float(j) * rates) if j else out
        line = jnp.sum(terms, axis=0, keepdims=True)
        table_ref[l, pl.ds(5 * modes + j, 1), cols] = line if j else line + skip


def section_kernel(
    highs, signal_ref, weight_ref, gain_in, step_in, mix_in, skip_in, out_ref,
    raw_ref, all_ref, cols_ref, first_ref, hidden_ref, x_ref, ends_ref, table_ref,
    gain_ref, step_ref, mix_ref, skip_ref, stats_ref, last_ref, states_ref, rounded_ref, sems
):
    part, place = lax.axis_index("parts"), lax.axis_index("tm")
    high, low = place // SPLIT, place % SPLIT
    depth, width = weight_ref.shape[0], cols_ref.shape[1]
    fine, channels = signal_ref.shape
    half = depth // 2
    cuts = 2 if half % 32 == 0 else 1
    cut = half // cuts
    own_rows = fine // POOL
    rows = own_rows * SPLIT
    piece = own_rows // PIECES
    chunk = SPLIT * depth
    groups = width // LANES
    layers, modes = mix_ref.shape[0], mix_ref.shape[1]
    blocks = rows // BLOCK
    last_step = highs - 1
    other = 1 - part
    exact = lax.Precision.HIGHEST
    (near_send, near_recv, own_sem, line_send, line_recv, side_send, side_recv, rows_send, rows_recv,
     stats_send, stats_recv, state_send, state_recv, out_send, out_recv, extra_send, extra_recv) = sems
    flip = lambda bit: low + bit - 2 * bit * ((low // bit) % 2)
    core, cross, diagonal = flip(1), flip(2), SPLIT - 1 - low
    near_by = (core, cross, diagonal)
    queue = (low, core, cross, diagonal)
    at = lambda p, h, l: (p, h * SPLIT + l)
    own_cols = pl.ds(pl.multiple_of(low * width, width), width)

    own_copies = [
        pltpu.make_async_copy(signal_ref, raw_ref, own_sem.at[0]),
        pltpu.make_async_copy(
            weight_ref.at[:, own_cols],
            cols_ref.at[pl.ds(pl.multiple_of(high * chunk + low * depth, depth), depth), :],
            own_sem.at[1],
        ),
        pltpu.make_async_copy(gain_in.at[:, own_cols], gain_ref, own_sem.at[2]),
        pltpu.make_async_copy(step_in.at[:, own_cols], step_ref, own_sem.at[3]),
        pltpu.make_async_copy(mix_in.at[:, :, own_cols], mix_ref, own_sem.at[4]),
        pltpu.make_async_copy(skip_in.at[:, own_cols], skip_ref, own_sem.at[5]),
    ]
    for copy in own_copies:
        copy.start()

    barrier = pltpu.get_barrier_semaphore()

    def greet(device):
        pl.semaphore_signal(barrier, inc=1, device_id=device, device_id_type=MESH)

    for who in near_by:
        greet(at(part, high, who))
    greet(at(other, high, low))

    def greet_high(h, carry):
        pl.when(h != high)(lambda: greet(at(part, h, low)))
        return carry

    pl.when(high > 0)(lambda: greet(at(part, high - 1, low)))
    pl.when(high < highs - 1)(lambda: greet(at(part, high + 1, low)))
    pl.semaphore_wait(barrier, 4 + jnp.minimum(high, 1) + jnp.minimum(highs - 1 - high, 1))

    def spot(h, l, which, c):
        start = pl.multiple_of(h * chunk + l * depth + which * half + c * cut, cut)
        return cols_ref.at[pl.ds(start, cut), :]

    def source(to, which, c):
        return weight_ref.at[
            pl.ds(pl.multiple_of(which * half + c * cut, cut), cut),
            pl.ds(pl.multiple_of(to * width, width), width),
        ]

    def near(bit, which, c):
        to = near_by[bit]
        return pltpu.make_async_remote_copy(
            source(to, which, c), spot(high, low, which, c), near_send.at[bit, which, c],
            near_recv.at[bit, which, c], device_id=at(part, high, to), device_id_type=MESH,
        )

    def near_arrived(bit, which, c):
        where = spot(high, near_by[bit], which, c)
        pltpu.make_async_remote_copy(
            where, where, near_send.at[bit, which, c], near_recv.at[bit, which, c],
            device_id=at(part, high, near_by[bit]), device_id_type=MESH,
        ).wait_recv()

    def line(up, h, l, c, own=False):
        to = jnp.clip(high + (1 if up else -1), 0, highs - 1)
        return pltpu.make_async_remote_copy(
            source(low, part, c) if own else spot(h, l, part, c), spot(h, l, part, c),
            line_send.at[int(up), h, l, c], line_recv.at[h, l, c],
            device_id=at(part, to, low), device_id_type=MESH,
        )

    def both_ways(l, c, own=False):
        pl.when(high < highs - 1)(lambda: line(True, high, l, c, own).start())
        pl.when(high > 0)(lambda: line(False, high, l, c, own).start())

    def side(h, l, which, c):
        return pltpu.make_async_remote_copy(
            spot(h, l, which, c), spot(h, l, which, c), side_send.at[h, l, c], side_recv.at[h, l, c],
            device_id=at(other, high, low), device_id_type=MESH,
        )

    def block(owner, p):
        start = pl.multiple_of(owner * own_rows + p * piece, piece)
        return all_ref.at[pl.ds(start, piece), :]

    def give(bit, p):
        return pltpu.make_async_remote_copy(
            block(low, p), block(low, p), rows_send.at[bit, p], rows_recv.at[bit, p],
            device_id=at(part, high, near_by[bit]), device_id_type=MESH,
        )

    def taken(bit, p):
        where = block(near_by[bit], p)
        pltpu.make_async_remote_copy(
            where, where, rows_send.at[bit, p], rows_recv.at[bit, p],
            device_id=at(part, high, core), device_id_type=MESH,
        ).wait_recv()

    def pass_on(p):
        return pltpu.make_async_remote_copy(
            block(cross, p), block(cross, p), rows_send.at[2, p], rows_recv.at[2, p],
            device_id=at(part, high, core), device_id_type=MESH,
        )

    for c in range(cuts):
        both_ways(low, c, True)
    for bit in (1, 2, 0):
        for c in range(cuts):
            near(bit, part, c).start()
    near(2, other, cuts - 1).start()

    own_copies[0].wait()
    line_of = lax.broadcasted_iota(jnp.int32, (own_rows, fine), 0)
    tick = lax.broadcasted_iota(jnp.int32, (own_rows, fine), 1)
    own_start = pl.multiple_of(low * own_rows, own_rows)
    for q in range(POOL):
        pick = (tick == POOL * line_of + q).astype(jnp.bfloat16)
        picked = jnp.dot(pick, raw_ref[...], preferred_element_type=jnp.float32)
        all_ref[pl.ds(own_start, own_rows), pl.ds(q * channels, channels)] = picked.astype(jnp.bfloat16)

    for p in range(PIECES):
        give(1, p).start()
    for p in range(PIECES):
        give(0, p).start()
    for bit in (1, 2, 0):
        for c in range(cuts if bit != 2 else cuts - 1):
            near(bit, other, c).start()
    for c in range(cuts):
        near_arrived(0, part, c)
        both_ways(core, c)

    for copy in own_copies[1:]:
        copy.wait()

    def lanes(g):
        return pl.ds(pl.multiple_of(g * LANES, LANES), LANES)

    def tables_of(l):
        def one(g, carry):
            make_tables(l, lanes(g), rows, step_ref, mix_ref, skip_ref, table_ref)
            return carry

        lax.fori_loop(0, groups, one, 0)

    tables_of(0)

    def by_side(h, k, c):
        if k == SPLIT - 1 and c == cuts - 1:
            return (h > 0) & (h < highs - 1)
        return True

    def extra(up):
        h = 0 if up else highs - 1
        to = jnp.clip(high + (1 if up else -1), 0, highs - 1)
        where = spot(h, diagonal, other, cuts - 1)
        return pltpu.make_async_remote_copy(
            where, where, extra_send.at[int(up)], extra_recv.at[int(up)],
            device_id=at(part, to, low), device_id_type=MESH,
        )

    def incoming(s):
        return (
            (True, high - s, high - s >= 0, high < highs - 1),
            (False, high + s, high + s < highs, high > 0),
        )

    def arrive(s, k, c):
        for up, h, there, _ in incoming(s):
            @pl.when(there)
            def _(up=up, h=h):
                line(up, h, queue[k], c).wait_recv()
                side(h, queue[k], part, c).start()

    def forward(s, k, c):
        for up, h, there, more in incoming(s):
            pl.when(there & more)(lambda: line(up, h, queue[k], c).start())

    def relay(s, k, c):
        for up, h, there, more in incoming(s):
            @pl.when(there)
            def _(up=up, h=h, more=more):
                line(up, h, queue[k], c).wait_recv()
                pl.when(more)(lambda: line(up, h, queue[k], c).start())
                if by_side(h, k, c) is True:
                    side(h, queue[k], part, c).start()
                else:
                    inner = by_side(h, k, c)
                    pl.when(inner)(lambda: side(h, queue[k], part, c).start())

                    @pl.when(jnp.logical_not(inner))
                    def _():
                        extra(up).wait_recv()
                        pl.when(more)(lambda: extra(up).start())

    def rows_on(p):
        taken(1, p)
        pass_on(p).start()

    for c in range(cuts):
        arrive(1, 0, c)
    for c in range(cuts):
        near_arrived(1, part, c)
        both_ways(cross, c)
        arrive(1, 1, c)
    for c in range(cuts):
        near_arrived(2, part, c)
        both_ways(diagonal, c)
    for k in (0, 1):
        for c in range(cuts):
            forward(1, k, c)
    for c in range(cuts):
        relay(1, 2, c)
    near_arrived(2, other, cuts - 1)
    pl.when(high == 0)(lambda: extra(True).start())
    pl.when(high == highs - 1)(lambda: extra(False).start())
    for layer in range(1, layers):
        tables_of(layer)
    for c in range(cuts):
        relay(1, 3, c)
    rows_on(0)

    def step(s, carry):
        for k in (0, 1):
            for c in range(cuts):
                relay(s, k, c)
        pl.when(s == 2)(lambda: rows_on(1))
        for k in (2, 3):
            for c in range(cuts):
                relay(s, k, c)
        pl.when(s == 2)(lambda: rows_on(2))
        return carry

    lax.fori_loop(2, last_step, step, 0)

    def multiply(start, size):
        start = pl.multiple_of(start, size)
        return jnp.dot(
            all_ref[:, pl.ds(start, size)], cols_ref[pl.ds(start, size), :],
            preferred_element_type=jnp.float32,
        )

    def keep(value, fresh):
        for g in range(groups):
            piece_of = value[:, g * LANES : (g + 1) * LANES]
            first_ref[g] = piece_of if fresh else first_ref[g] + piece_of

    def side_arrived(h, k):
        for c in range(cuts):
            if by_side(h, k, c) is True:
                side(h, queue[k], other, c).wait_recv()
            else:
                pl.when(by_side(h, k, c))(lambda: side(h, queue[k], other, c).wait_recv())

    def add(s, carry):
        for h, there in ((high - s, high - s >= 0), (high + s, high + s < highs)):
            @pl.when(there)
            def _(h=h):
                for k in range(SPLIT):
                    side_arrived(h, k)
                keep(multiply(h * chunk, chunk), False)

        return carry

    def add_each(s, carry):
        if depth % LANES:
            return add(s, carry)

        for h, there in ((high - s, high - s >= 0), (high + s, high + s < highs)):
            @pl.when(there)
            def _(h=h):
                for k in range(SPLIT):
                    side_arrived(h, k)
                    keep(multiply(h * chunk + queue[k] * depth, depth), False)

        return carry

    for k in (0, 1):
        for c in range(cuts):
            relay(last_step, k, c)
    rows_on(3)
    relay(last_step, 2, 0)
    first_ref[...] = jnp.zeros_like(first_ref)
    for p in range(PIECES):
        taken(0, p)
        taken(2, p)
    add(1, 0)
    for c in range(1, cuts):
        relay(last_step, 2, c)
    for c in range(cuts):
        relay(last_step, 3, c)
    lax.fori_loop(2, last_step, add_each, 0)
    for bit in range(3):
        for c in range(cuts if bit != 2 else cuts - 1):
            near_arrived(bit, other, c)
    keep(multiply(high * chunk, chunk), False)
    add_each(last_step, 0)

    def pool_sent():
        for bit in range(3):
            for c in range(cuts):
                near(bit, 0, c).wait_send()
                near(bit, 1, c).wait_send()
        for p in range(PIECES):
            give(0, p).wait_send()
            give(1, p).wait_send()
            pass_on(p).wait_send()

        def sent(h, carry):
            for k, l in enumerate(queue):
                for c in range(cuts):
                    pl.when((h <= high) & (high < highs - 1))(lambda: line(True, h, l, c).wait_send())
                    pl.when((h >= high) & (high > 0))(lambda: line(False, h, l, c).wait_send())
                    pl.when((h != high) & by_side(h, k, c))(lambda: side(h, l, part, c).wait_send())
            return carry

        lax.fori_loop(0, highs, sent, 0)
        pl.when(high < highs - 1)(lambda: extra(True).wait_send())
        pl.when(high > 0)(lambda: extra(False).wait_send())

    def stats_copy(l, part_of, bit, owner):
        return pltpu.make_async_remote_copy(
            stats_ref.at[l, part_of, owner], stats_ref.at[l, part_of, owner],
            stats_send.at[l, part_of, bit], stats_recv.at[l, part_of, bit],
            device_id=at(part, high, near_by[bit]), device_id_type=MESH,
        )

    def state_copy(l, g, origin, target):
        return pltpu.make_async_remote_copy(
            last_ref.at[l, g], states_ref.at[l, origin, g], state_send.at[l, target, g],
            state_recv.at[l, origin, g], device_id=at(part, target, low), device_id_type=MESH,
        )

    def out_cols(owner, g):
        return pl.ds(pl.multiple_of(owner * width + g * LANES, LANES), LANES)

    def out_copy(g, bit, owner):
        start = pl.multiple_of(near_by[bit] * own_rows, own_rows)
        return pltpu.make_async_remote_copy(
            rounded_ref.at[g, pl.ds(start, own_rows), :], out_ref.at[:, out_cols(owner, g)],
            out_send.at[g, bit], out_recv.at[g, bit],
            device_id=at(part, high, near_by[bit]), device_id_type=MESH,
        )

    def own_out(g):
        return pltpu.make_async_copy(
            rounded_ref.at[g, pl.ds(own_start, own_rows), :], out_ref.at[:, out_cols(low, g)], own_sem.at[6 + g]
        )

    spans = rows // (2 * LANES)
    half_rows = spans * LANES
    sub = lax.broadcasted_iota(jnp.int32, (2 * spans, LANES), 0)
    state_of = lambda l: first_ref if l == 0 else hidden_ref

    def fold(wide):
        folded = wide[:, 0:LANES]
        for i in range(1, spans):
            folded = jnp.where(sub % spans == i, wide[:, i * LANES : (i + 1) * LANES], folded)
        return folded

    def stats(l, part_of):
        source_ref = state_of(l)
        rows_of = pl.ds(part_of * half_rows, half_rows)
        values = [source_ref[g, rows_of, :] for g in range(groups)]
        total = values[0]
        for value in values[1:]:
            total = total + value
        mean = jnp.sum(total, axis=-1, keepdims=True) / width
        square = jnp.square(values[0] - mean)
        for value in values[1:]:
            square = square + jnp.square(value - mean)
        ones = jnp.ones((2 * spans, LANES), jnp.float32)
        across = lambda v: lax.dot_general(
            ones, v, (((1,), (1,)), ((), ())), precision=exact, preferred_element_type=jnp.float32
        )
        folded = jnp.where(sub < spans, fold(across(total)) / width, fold(across(square)))
        stats_ref[l, part_of, low, pl.ds(0, 2 * spans), :] = folded
        for bit in (1, 2, 0):
            stats_copy(l, part_of, bit, low).start()

    def moments(l, part_of):
        for bit in range(3):
            stats_copy(l, part_of, bit, near_by[bit]).wait_recv()
        every = [stats_ref[l, part_of, i, pl.ds(0, 2 * spans), :] for i in range(SPLIT)]
        means = [e[0:spans] for e in every]
        row_mean = (means[0] + means[1] + means[2] + means[3]) / SPLIT
        row_var = sum(e[spans : 2 * spans] + width * jnp.square(e[0:spans] - row_mean) for e in every)
        row_scale = lax.rsqrt(row_var / (width * SPLIT) + 1e-05)
        return jnp.transpose(jnp.concatenate([row_mean, row_scale] * (8 // (2 * spans)), axis=0))

    def normalize(l, part_of, both, g):
        gain = gain_ref[pl.ds(l, 1), lanes(g)]
        for i in range(spans):
            where = pl.ds(part_of * half_rows + i * LANES, LANES)
            x_ref[g, where, :] = (
                (state_of(l)[g, where, :] - both[:, i : i + 1]) * both[:, spans + i : spans + i + 1] * gain
            )

    stats(0, 0)
    stats(0, 1)
    pool_sent()

    for l in range(layers):
        source_ref = state_of(l)
        final = l == layers - 1
        whole_spans = rows // (8 * BLOCK)
        half_spans = whole_spans // 2
        early = 1 - low // 2 if final else 0

        def table(index, g, size):
            return table_ref.at[l, pl.ds(index * modes, size), lanes(g)]

        cols = slice(None)
        eights = modes // 8

        def send(g):
            def one(h, carry):
                pl.when(h > high)(lambda: state_copy(l, g, high, h).start())
                return carry

            lax.fori_loop(1, highs, one, 0)

        both = moments(l, 0)
        for g in range(groups):
            normalize(l, 0, both, g)

        def ends_first(g, carry):
            block_ends(
                x_ref.at[g], table(0, g, modes), ends_ref.at[g], modes, cols, 0, half_spans
            )
            return carry

        lax.fori_loop(0, groups, ends_first, 0)
        both = moments(l, 1)
        for g in range(groups):
            normalize(l, 1, both, g)

        def ends(g, carry):
            block_ends(
                x_ref.at[g], table(0, g, modes), ends_ref.at[g], modes, cols, half_spans, half_spans
            )
            zero = [jnp.zeros((8, LANES), jnp.float32)] * eights
            last = scan_blocks(blocks, ends_ref.at[g], table(1, g, modes), modes, cols, zero)
            for i in range(eights):
                last_ref[l, g, pl.ds(i * 8, 8), :] = last[i]
            send(g)
            return carry

        lax.fori_loop(0, groups, ends, 0)

        def answer(g, which):
            respond(
                x_ref.at[g], source_ref.at[g], ends_ref.at[g], table(4, g, BLOCK),
                table(5, g, BLOCK), hidden_ref.at[g], modes, cols, which * half_spans, half_spans,
            )
            if final:
                where = pl.ds(pl.multiple_of(which * half_rows, half_rows), half_rows)
                rounded_ref[g, where, :] = hidden_ref[g, where, :].astype(jnp.bfloat16)

        def finish(g, carry):
            whole = table(2, g, modes)

            def join(h, start):
                @pl.when(h < high)
                def _():
                    state_copy(l, g, h, high).wait_recv()
                    states_ref[l, high, g] = whole[...] * states_ref[l, high, g] + states_ref[l, h, g]
                return start

            states_ref[l, high, g] = jnp.zeros((modes, LANES), jnp.float32)
            lax.fori_loop(0, highs - 1, join, 0)
            start = [states_ref[l, high, g, pl.ds(i * 8, 8), :] for i in range(eights)]
            scan_blocks(
                blocks, ends_ref.at[g], table(1, g, modes), modes, cols, start, table(3, g, modes)
            )
            answer(g, early)
            if final:
                for bit in (1, 2):
                    out_copy(g, bit, low).start()
            return carry

        lax.fori_loop(0, groups, finish, 0)
        if not final:
            stats(l + 1, 0)

        def finish_rest(g, carry):
            answer(g, 1 - early)
            if final:
                out_copy(g, 0, low).start()
                own_out(g).start()
            return carry

        lax.fori_loop(0, groups, finish_rest, 0)
        if not final:
            stats(l + 1, 1)

    def drain(g, carry):
        own_out(g).wait()
        for bit in range(3):
            out_copy(g, bit, near_by[bit]).wait_recv()
            out_copy(g, bit, low).wait_send()

        def one(h, carry):
            @pl.when(h > high)
            def _():
                for l in range(layers):
                    state_copy(l, g, high, h).wait_send()
            return carry

        return lax.fori_loop(1, highs, one, carry)

    for l in range(layers):
        for part_of in range(2):
            for bit in range(3):
                stats_copy(l, part_of, bit, low).wait_send()
    lax.fori_loop(0, groups, drain, 0)


def local(signal, pool_weight, norm_gain, step_size, mode_out, skip_gain):
    fine, channels = signal.shape
    depth, total = pool_weight.shape
    layers, modes, _ = mode_out.shape
    own_rows = fine // POOL
    rows = own_rows * SPLIT
    width = total // SPLIT
    groups = width // LANES
    highs = lax.axis_size("tm") // SPLIT
    cuts = 2 if depth % 64 == 0 else 1
    dma = pltpu.SemaphoreType.DMA
    vmem, f32, b16 = pltpu.VMEM, jnp.float32, jnp.bfloat16
    anywhere = pl.BlockSpec(memory_space=pl.ANY)
    far = pl.BlockSpec(memory_space=pltpu.HBM)
    return pl.pallas_call(
        functools.partial(section_kernel, highs),
        out_shape=jax.ShapeDtypeStruct((own_rows, total), b16),
        in_specs=[far] * 6,
        out_specs=anywhere,
        scratch_shapes=[
            vmem((fine, channels), b16),
            vmem((rows, POOL * channels), b16),
            vmem((POOL * channels, width), b16),
            vmem((groups, rows, LANES), f32),
            vmem((groups, rows, LANES), f32),
            vmem((groups, rows, LANES), f32),
            vmem((groups, (modes + PAD) * (rows // BLOCK), LANES), f32),
            vmem((layers, 6 * modes, width), f32),
            vmem((layers, width), f32),
            vmem((layers, width), f32),
            vmem((layers, modes, width), f32),
            vmem((layers, width), f32),
            vmem((layers, 2, SPLIT, 8, LANES), f32),
            vmem((layers, groups, modes, LANES), f32),
            vmem((layers, highs, groups, modes, LANES), f32),
            vmem((groups, rows, LANES), b16),
            [
                dma((3, 2, cuts)), dma((3, 2, cuts)), dma((6 + groups,)),
                dma((2, highs, SPLIT, cuts)), dma((highs, SPLIT, cuts)),
                dma((highs, SPLIT, cuts)), dma((highs, SPLIT, cuts)),
                dma((3, PIECES)), dma((3, PIECES)),
                dma((layers, 2, 3)), dma((layers, 2, 3)), dma((layers, highs, groups)),
                dma((layers, highs, groups)), dma((groups, 3)), dma((groups, 3)), dma((2,)), dma((2,)),
            ],
        ],
        compiler_params=pltpu.CompilerParams(
            collective_id=0, has_side_effects=True, vmem_limit_bytes=57000000
        ),
    )(signal, pool_weight, norm_gain, step_size, mode_out, skip_gain)


def solution(mesh):
    placed = (P(("parts", "tm"), None), P("tm", None), P(), P(), P(), P())
    return jax.shard_map(
        local, mesh=mesh, in_specs=placed, out_specs=P(("parts", "tm"), None), check_vma=False
    )
```

```python
import functools

import jax
import jax.numpy as jnp
from jax import lax
from jax.experimental import pallas as pl
from jax.experimental.pallas import tpu as pltpu
from jax.sharding import PartitionSpec as P

POOL = 4
SPLIT = 4
BLOCK = 16
LANES = 128
PIECES = 4
PAD = 1


def block_ends(x_ref, decay_ref, ends_ref, modes, cols, first, count):
    blocks = x_ref.shape[0] // BLOCK
    span = 8 * BLOCK
    pitch = ends_ref.shape[0] // blocks

    def group(g, carry):
        base = pl.multiple_of(g * span, span)
        xs = [x_ref[pl.ds(base + j, 8, stride=BLOCK), cols] for j in range(BLOCK)]
        for n in range(modes):
            decay = jnp.broadcast_to(decay_ref[pl.ds(n, 1), cols], (8, LANES))
            end = xs[0]
            for j in range(1, BLOCK):
                end = end * decay + xs[j]
            ends_ref[pl.ds(g * 8 * pitch + n, 8, stride=pitch), cols] = end
        return carry

    lax.fori_loop(first, first + count, group, 0)


def scan_blocks(blocks, ends_ref, step_ref, modes, cols, start, out_ref=None):
    pitch = ends_ref.shape[0] // blocks
    groups = modes // 8
    steps = [step_ref[pl.ds(i * 8, 8), cols] for i in range(groups)]
    outs = [out_ref[pl.ds(i * 8, 8), cols] for i in range(groups)] if out_ref is not None else None
    states = list(start)
    for b in range(blocks):
        for i in range(groups):
            where = pl.ds(b * pitch + i * 8, 8)
            end = ends_ref[where, cols]
            if outs is not None:
                ends_ref[where, cols] = states[i] * outs[i]
            states[i] = states[i] * steps[i] + end
    return states


def respond(
    x_ref, hidden_ref, ends_ref, powers_ref, kernel_ref, result_ref, modes, cols, first, count
):
    blocks = x_ref.shape[0] // BLOCK
    span = 8 * BLOCK
    pitch = ends_ref.shape[0] // blocks

    def group(g, carry):
        base = pl.multiple_of(g * span, span)
        coefs = [ends_ref[pl.ds(g * 8 * pitch + n, 8, stride=pitch), cols] for n in range(modes)]
        xs = [x_ref[pl.ds(base + j, 8, stride=BLOCK), cols] for j in range(BLOCK)]
        for j in range(BLOCK):
            power = jnp.broadcast_to(powers_ref[pl.ds(j, 1), cols], (8, LANES))
            total = coefs[modes - 1]
            for n in range(modes - 2, -1, -1):
                total = total * power + coefs[n]
            total = total * power
            for i in range(j + 1):
                total = total + xs[i] * jnp.broadcast_to(
                    kernel_ref[pl.ds(j - i, 1), cols], (8, LANES)
                )
            where = pl.ds(base + j, 8, stride=BLOCK)
            gelu = 0.5 * total * (1.0 + lax.erf(total * 0.7071067811865476))
            result_ref[where, cols] = hidden_ref[where, cols] + gelu
        return carry

    lax.fori_loop(first, first + count, group, 0)


MESH = pl.DeviceIdType.MESH


def decay_left(y):
    small = jnp.ones_like(y)
    for k in range(10, 1, -1):
        small = 1.0 - y * (1.0 / k) * small
    return jnp.where(y < 0.5, y * small, 1.0 - jnp.exp(-y))


def make_tables(l, cols, rows, step_ref, mix_ref, skip_ref, table_ref):
    modes = mix_ref.shape[1]
    step = step_ref[pl.ds(l, 1), cols]
    order = lax.broadcasted_iota(jnp.int32, (modes, LANES), 0).astype(jnp.float32) + 1.0
    rates = jnp.broadcast_to(step, (modes, LANES)) * order
    out = mix_ref[l, :, cols] * jnp.sqrt(decay_left(2.0 * rates))
    table_ref[l, pl.ds(0, modes), cols] = jnp.exp(-rates)
    table_ref[l, pl.ds(modes, modes), cols] = jnp.exp(-rates * BLOCK)
    table_ref[l, pl.ds(2 * modes, modes), cols] = jnp.exp(-rates * rows)
    table_ref[l, pl.ds(3 * modes, modes), cols] = out
    lags = lax.broadcasted_iota(jnp.int32, (BLOCK, LANES), 0).astype(jnp.float32) + 1.0
    table_ref[l, pl.ds(4 * modes, BLOCK), cols] = jnp.exp(-lags * jnp.broadcast_to(step, (BLOCK, LANES)))
    skip = skip_ref[pl.ds(l, 1), cols]
    for j in range(BLOCK):
        terms = out * jnp.exp(-float(j) * rates) if j else out
        line = jnp.sum(terms, axis=0, keepdims=True)
        table_ref[l, pl.ds(5 * modes + j, 1), cols] = line if j else line + skip


def section_kernel(
    highs, signal_ref, weight_ref, gain_in, step_in, mix_in, skip_in, out_ref,
    raw_ref, all_ref, cols_ref, first_ref, hidden_ref, x_ref, ends_ref, table_ref,
    gain_ref, step_ref, mix_ref, skip_ref, stats_ref, last_ref, states_ref, rounded_ref, sems
):
    part, place = lax.axis_index("parts"), lax.axis_index("tm")
    high, low = place // SPLIT, place % SPLIT
    depth, width = weight_ref.shape[0], cols_ref.shape[1]
    fine, channels = signal_ref.shape
    half = depth // 2
    cuts = 2 if half % 32 == 0 else 1
    sizes = (half * 3 // 8 // 16 * 16, half - half * 3 // 8 // 16 * 16) if cuts == 2 else (half,)
    starts = (0, sizes[0])
    own_rows = fine // POOL
    rows = own_rows * SPLIT
    piece = own_rows // PIECES
    chunk = SPLIT * depth
    groups = width // LANES
    layers, modes = mix_ref.shape[0], mix_ref.shape[1]
    blocks = rows // BLOCK
    last_step = highs - 1
    other = 1 - part
    exact = lax.Precision.HIGHEST
    (near_send, near_recv, own_sem, line_send, line_recv, side_send, side_recv, rows_send, rows_recv,
     stats_send, stats_recv, state_send, state_recv, out_send, out_recv, extra_send, extra_recv) = sems
    flip = lambda bit: low + bit - 2 * bit * ((low // bit) % 2)
    core, cross, diagonal = flip(1), flip(2), SPLIT - 1 - low
    near_by = (core, cross, diagonal)
    queue = (low, core, cross, diagonal)
    at = lambda p, h, l: (p, h * SPLIT + l)
    own_cols = pl.ds(pl.multiple_of(low * width, width), width)

    own_copies = [
        pltpu.make_async_copy(signal_ref, raw_ref, own_sem.at[0]),
        pltpu.make_async_copy(
            weight_ref.at[:, own_cols],
            cols_ref.at[pl.ds(pl.multiple_of(high * chunk + low * depth, depth), depth), :],
            own_sem.at[1],
        ),
        pltpu.make_async_copy(gain_in.at[:, own_cols], gain_ref, own_sem.at[2]),
        pltpu.make_async_copy(step_in.at[:, own_cols], step_ref, own_sem.at[3]),
        pltpu.make_async_copy(mix_in.at[:, :, own_cols], mix_ref, own_sem.at[4]),
        pltpu.make_async_copy(skip_in.at[:, own_cols], skip_ref, own_sem.at[5]),
    ]
    for copy in own_copies:
        copy.start()

    barrier = pltpu.get_barrier_semaphore()

    def greet(device):
        pl.semaphore_signal(barrier, inc=1, device_id=device, device_id_type=MESH)

    for who in near_by:
        greet(at(part, high, who))
    greet(at(other, high, low))

    def greet_high(h, carry):
        pl.when(h != high)(lambda: greet(at(part, h, low)))
        return carry

    pl.when(high > 0)(lambda: greet(at(part, high - 1, low)))
    pl.when(high < highs - 1)(lambda: greet(at(part, high + 1, low)))
    pl.semaphore_wait(barrier, 4 + jnp.minimum(high, 1) + jnp.minimum(highs - 1 - high, 1))

    def spot(h, l, which, c):
        start = pl.multiple_of(h * chunk + l * depth + which * half + starts[c], 16)
        return cols_ref.at[pl.ds(start, sizes[c]), :]

    def source(to, which, c):
        return weight_ref.at[
            pl.ds(pl.multiple_of(which * half + starts[c], 16), sizes[c]),
            pl.ds(pl.multiple_of(to * width, width), width),
        ]

    def near(bit, which, c):
        to = near_by[bit]
        return pltpu.make_async_remote_copy(
            source(to, which, c), spot(high, low, which, c), near_send.at[bit, which, c],
            near_recv.at[bit, which, c], device_id=at(part, high, to), device_id_type=MESH,
        )

    def near_arrived(bit, which, c):
        where = spot(high, near_by[bit], which, c)
        pltpu.make_async_remote_copy(
            where, where, near_send.at[bit, which, c], near_recv.at[bit, which, c],
            device_id=at(part, high, near_by[bit]), device_id_type=MESH,
        ).wait_recv()

    def line(up, h, l, c, own=False):
        to = jnp.clip(high + (1 if up else -1), 0, highs - 1)
        return pltpu.make_async_remote_copy(
            source(low, part, c) if own else spot(h, l, part, c), spot(h, l, part, c),
            line_send.at[int(up), h, l, c], line_recv.at[h, l, c],
            device_id=at(part, to, low), device_id_type=MESH,
        )

    def both_ways(l, c, own=False):
        pl.when(high < highs - 1)(lambda: line(True, high, l, c, own).start())
        pl.when(high > 0)(lambda: line(False, high, l, c, own).start())

    def side(h, l, which, c):
        return pltpu.make_async_remote_copy(
            spot(h, l, which, c), spot(h, l, which, c), side_send.at[h, l, c], side_recv.at[h, l, c],
            device_id=at(other, high, low), device_id_type=MESH,
        )

    def block(owner, p):
        start = pl.multiple_of(owner * own_rows + p * piece, piece)
        return all_ref.at[pl.ds(start, piece), :]

    def give(bit, p):
        return pltpu.make_async_remote_copy(
            block(low, p), block(low, p), rows_send.at[bit, p], rows_recv.at[bit, p],
            device_id=at(part, high, near_by[bit]), device_id_type=MESH,
        )

    def taken(bit, p):
        where = block(near_by[bit], p)
        pltpu.make_async_remote_copy(
            where, where, rows_send.at[bit, p], rows_recv.at[bit, p],
            device_id=at(part, high, core), device_id_type=MESH,
        ).wait_recv()

    def pass_on(p):
        return pltpu.make_async_remote_copy(
            block(cross, p), block(cross, p), rows_send.at[2, p], rows_recv.at[2, p],
            device_id=at(part, high, core), device_id_type=MESH,
        )

    for c in range(cuts):
        both_ways(low, c, True)
    for bit in (1, 2, 0):
        for c in range(cuts):
            near(bit, part, c).start()
    near(2, other, cuts - 1).start()

    own_copies[0].wait()
    line_of = lax.broadcasted_iota(jnp.int32, (own_rows, fine), 0)
    tick = lax.broadcasted_iota(jnp.int32, (own_rows, fine), 1)
    own_start = pl.multiple_of(low * own_rows, own_rows)
    for q in range(POOL):
        pick = (tick == POOL * line_of + q).astype(jnp.bfloat16)
        picked = jnp.dot(pick, raw_ref[...], preferred_element_type=jnp.float32)
        all_ref[pl.ds(own_start, own_rows), pl.ds(q * channels, channels)] = picked.astype(jnp.bfloat16)

    for p in range(PIECES):
        give(1, p).start()
    for p in range(PIECES):
        give(0, p).start()
    for bit in (1, 2, 0):
        for c in range(cuts if bit != 2 else cuts - 1):
            near(bit, other, c).start()
    for c in range(cuts):
        near_arrived(0, part, c)
        both_ways(core, c)

    for copy in own_copies[1:]:
        copy.wait()

    def lanes(g):
        return pl.ds(pl.multiple_of(g * LANES, LANES), LANES)

    def tables_of(l):
        def one(g, carry):
            make_tables(l, lanes(g), rows, step_ref, mix_ref, skip_ref, table_ref)
            return carry

        lax.fori_loop(0, groups, one, 0)

    tables_of(0)

    def by_side(h, k, c):
        if k == SPLIT - 1 and c == cuts - 1:
            return (h > 0) & (h < highs - 1)
        return True

    def extra(up):
        h = 0 if up else highs - 1
        to = jnp.clip(high + (1 if up else -1), 0, highs - 1)
        where = spot(h, diagonal, other, cuts - 1)
        return pltpu.make_async_remote_copy(
            where, where, extra_send.at[int(up)], extra_recv.at[int(up)],
            device_id=at(part, to, low), device_id_type=MESH,
        )

    def incoming(s):
        return (
            (True, high - s, high - s >= 0, high < highs - 1),
            (False, high + s, high + s < highs, high > 0),
        )

    def arrive(s, k, c):
        for up, h, there, _ in incoming(s):
            @pl.when(there)
            def _(up=up, h=h):
                line(up, h, queue[k], c).wait_recv()
                side(h, queue[k], part, c).start()

    def forward(s, k, c):
        for up, h, there, more in incoming(s):
            pl.when(there & more)(lambda: line(up, h, queue[k], c).start())

    def relay(s, k, c):
        for up, h, there, more in incoming(s):
            @pl.when(there)
            def _(up=up, h=h, more=more):
                line(up, h, queue[k], c).wait_recv()
                pl.when(more)(lambda: line(up, h, queue[k], c).start())
                if by_side(h, k, c) is True:
                    side(h, queue[k], part, c).start()
                else:
                    inner = by_side(h, k, c)
                    pl.when(inner)(lambda: side(h, queue[k], part, c).start())

                    @pl.when(jnp.logical_not(inner))
                    def _():
                        extra(up).wait_recv()
                        pl.when(more)(lambda: extra(up).start())

    def rows_on(p):
        taken(1, p)
        pass_on(p).start()

    for c in range(cuts):
        arrive(1, 0, c)
    for c in range(cuts):
        near_arrived(1, part, c)
        both_ways(cross, c)
        arrive(1, 1, c)
    for c in range(cuts):
        near_arrived(2, part, c)
        both_ways(diagonal, c)
    for k in (0, 1):
        for c in range(cuts):
            forward(1, k, c)
    for c in range(cuts):
        relay(1, 2, c)
    near_arrived(2, other, cuts - 1)
    pl.when(high == 0)(lambda: extra(True).start())
    pl.when(high == highs - 1)(lambda: extra(False).start())
    for layer in range(1, layers):
        tables_of(layer)
    for c in range(cuts):
        relay(1, 3, c)
    rows_on(0)

    def step(s, carry):
        for k in (0, 1):
            for c in range(cuts):
                relay(s, k, c)
        pl.when(s == 2)(lambda: rows_on(1))
        for k in (2, 3):
            for c in range(cuts):
                relay(s, k, c)
        pl.when(s == 2)(lambda: rows_on(2))
        return carry

    lax.fori_loop(2, last_step, step, 0)

    def multiply(start, size):
        start = pl.multiple_of(start, size)
        return jnp.dot(
            all_ref[:, pl.ds(start, size)], cols_ref[pl.ds(start, size), :],
            preferred_element_type=jnp.float32,
        )

    def keep(value, fresh):
        for g in range(groups):
            piece_of = value[:, g * LANES : (g + 1) * LANES]
            first_ref[g] = piece_of if fresh else first_ref[g] + piece_of

    def side_arrived(h, k):
        for c in range(cuts):
            if by_side(h, k, c) is True:
                side(h, queue[k], other, c).wait_recv()
            else:
                pl.when(by_side(h, k, c))(lambda: side(h, queue[k], other, c).wait_recv())

    def add(s, carry):
        for h, there in ((high - s, high - s >= 0), (high + s, high + s < highs)):
            @pl.when(there)
            def _(h=h):
                for k in range(SPLIT):
                    side_arrived(h, k)
                keep(multiply(h * chunk, chunk), False)

        return carry

    def add_each(s, carry):
        if depth % LANES:
            return add(s, carry)

        for h, there in ((high - s, high - s >= 0), (high + s, high + s < highs)):
            @pl.when(there)
            def _(h=h):
                for k in range(SPLIT):
                    side_arrived(h, k)
                    keep(multiply(h * chunk + queue[k] * depth, depth), False)

        return carry

    for k in (0, 1):
        for c in range(cuts):
            relay(last_step, k, c)
    rows_on(3)
    relay(last_step, 2, 0)
    first_ref[...] = jnp.zeros_like(first_ref)
    for p in range(PIECES):
        taken(0, p)
        taken(2, p)
    add(1, 0)
    for c in range(1, cuts):
        relay(last_step, 2, c)
    at_end = (high == 0) | (high == highs - 1)

    @pl.when(at_end)
    def _():
        lax.fori_loop(2, last_step, add, 0)

    for c in range(cuts):
        relay(last_step, 3, c)
    for bit in range(3):
        for c in range(cuts if bit != 2 else cuts - 1):
            near_arrived(bit, other, c)
    keep(multiply(high * chunk, chunk), False)

    @pl.when(jnp.logical_not(at_end))
    def _():
        lax.fori_loop(2, last_step, add_each, 0)

    add_each(last_step, 0)

    def pool_sent():
        for bit in range(3):
            for c in range(cuts):
                near(bit, 0, c).wait_send()
                near(bit, 1, c).wait_send()
        for p in range(PIECES):
            give(0, p).wait_send()
            give(1, p).wait_send()
            pass_on(p).wait_send()

        def sent(h, carry):
            for k, l in enumerate(queue):
                for c in range(cuts):
                    pl.when((h <= high) & (high < highs - 1))(lambda: line(True, h, l, c).wait_send())
                    pl.when((h >= high) & (high > 0))(lambda: line(False, h, l, c).wait_send())
                    pl.when((h != high) & by_side(h, k, c))(lambda: side(h, l, part, c).wait_send())
            return carry

        lax.fori_loop(0, highs, sent, 0)
        pl.when(high < highs - 1)(lambda: extra(True).wait_send())
        pl.when(high > 0)(lambda: extra(False).wait_send())

    def stats_copy(l, part_of, bit, owner):
        return pltpu.make_async_remote_copy(
            stats_ref.at[l, part_of, owner], stats_ref.at[l, part_of, owner],
            stats_send.at[l, part_of, bit], stats_recv.at[l, part_of, bit],
            device_id=at(part, high, near_by[bit]), device_id_type=MESH,
        )

    def state_copy(l, g, origin, target):
        return pltpu.make_async_remote_copy(
            last_ref.at[l, g], states_ref.at[l, origin, g], state_send.at[l, target, g],
            state_recv.at[l, origin, g], device_id=at(part, target, low), device_id_type=MESH,
        )

    def out_cols(owner, g):
        return pl.ds(pl.multiple_of(owner * width + g * LANES, LANES), LANES)

    def out_copy(g, bit, owner):
        start = pl.multiple_of(near_by[bit] * own_rows, own_rows)
        return pltpu.make_async_remote_copy(
            rounded_ref.at[g, pl.ds(start, own_rows), :], out_ref.at[:, out_cols(owner, g)],
            out_send.at[g, bit], out_recv.at[g, bit],
            device_id=at(part, high, near_by[bit]), device_id_type=MESH,
        )

    def own_out(g):
        return pltpu.make_async_copy(
            rounded_ref.at[g, pl.ds(own_start, own_rows), :], out_ref.at[:, out_cols(low, g)], own_sem.at[6 + g]
        )

    spans = rows // (2 * LANES)
    half_rows = spans * LANES
    sub = lax.broadcasted_iota(jnp.int32, (2 * spans, LANES), 0)
    state_of = lambda l: first_ref if l == 0 else hidden_ref

    def fold(wide):
        folded = wide[:, 0:LANES]
        for i in range(1, spans):
            folded = jnp.where(sub % spans == i, wide[:, i * LANES : (i + 1) * LANES], folded)
        return folded

    def stats(l, part_of):
        source_ref = state_of(l)
        rows_of = pl.ds(part_of * half_rows, half_rows)
        values = [source_ref[g, rows_of, :] for g in range(groups)]
        total = values[0]
        for value in values[1:]:
            total = total + value
        mean = jnp.sum(total, axis=-1, keepdims=True) / width
        square = jnp.square(values[0] - mean)
        for value in values[1:]:
            square = square + jnp.square(value - mean)
        ones = jnp.ones((2 * spans, LANES), jnp.float32)
        across = lambda v: lax.dot_general(
            ones, v, (((1,), (1,)), ((), ())), precision=exact, preferred_element_type=jnp.float32
        )
        folded = jnp.where(sub < spans, fold(across(total)) / width, fold(across(square)))
        stats_ref[l, part_of, low, pl.ds(0, 2 * spans), :] = folded
        for bit in (1, 2, 0):
            stats_copy(l, part_of, bit, low).start()

    def moments(l, part_of):
        for bit in range(3):
            stats_copy(l, part_of, bit, near_by[bit]).wait_recv()
        every = [stats_ref[l, part_of, i, pl.ds(0, 2 * spans), :] for i in range(SPLIT)]
        means = [e[0:spans] for e in every]
        row_mean = (means[0] + means[1] + means[2] + means[3]) / SPLIT
        row_var = sum(e[spans : 2 * spans] + width * jnp.square(e[0:spans] - row_mean) for e in every)
        row_scale = lax.rsqrt(row_var / (width * SPLIT) + 1e-05)
        return jnp.transpose(jnp.concatenate([row_mean, row_scale] * (8 // (2 * spans)), axis=0))

    def normalize(l, part_of, both, g):
        gain = gain_ref[pl.ds(l, 1), lanes(g)]
        for i in range(spans):
            where = pl.ds(part_of * half_rows + i * LANES, LANES)
            x_ref[g, where, :] = (
                (state_of(l)[g, where, :] - both[:, i : i + 1]) * both[:, spans + i : spans + i + 1] * gain
            )

    stats(0, 0)
    stats(0, 1)
    pool_sent()

    for l in range(layers):
        source_ref = state_of(l)
        final = l == layers - 1
        whole_spans = rows // (8 * BLOCK)
        half_spans = whole_spans // 2

        def table(index, g, size):
            return table_ref.at[l, pl.ds(index * modes, size), lanes(g)]

        cols = slice(None)
        eights = modes // 8

        def send(g):
            def one(h, carry):
                pl.when(h > high)(lambda: state_copy(l, g, high, h).start())
                return carry

            lax.fori_loop(1, highs, one, 0)

        both = moments(l, 0)
        for g in range(groups):
            normalize(l, 0, both, g)

        def ends_first(g, carry):
            block_ends(
                x_ref.at[g], table(0, g, modes), ends_ref.at[g], modes, cols, 0, half_spans
            )
            return carry

        lax.fori_loop(0, groups, ends_first, 0)
        both = moments(l, 1)
        for g in range(groups):
            normalize(l, 1, both, g)

        def ends(g, carry):
            block_ends(
                x_ref.at[g], table(0, g, modes), ends_ref.at[g], modes, cols, half_spans, half_spans
            )
            zero = [jnp.zeros((8, LANES), jnp.float32)] * eights
            last = scan_blocks(blocks, ends_ref.at[g], table(1, g, modes), modes, cols, zero)
            for i in range(eights):
                last_ref[l, g, pl.ds(i * 8, 8), :] = last[i]
            send(g)
            return carry

        lax.fori_loop(0, groups, ends, 0)

        def answer(g, first, count):
            respond(
                x_ref.at[g], source_ref.at[g], ends_ref.at[g], table(4, g, BLOCK),
                table(5, g, BLOCK), hidden_ref.at[g], modes, cols, first, count,
            )

        def deliver(g, bit):
            owner = low if bit is None else near_by[bit]
            answer(g, owner * (whole_spans // SPLIT), whole_spans // SPLIT)
            where = pl.ds(pl.multiple_of(owner * own_rows, own_rows), own_rows)
            rounded_ref[g, where, :] = hidden_ref[g, where, :].astype(jnp.bfloat16)
            (own_out(g) if bit is None else out_copy(g, bit, low)).start()

        def finish(g, carry):
            whole = table(2, g, modes)

            def join(h, start):
                @pl.when(h < high)
                def _():
                    state_copy(l, g, h, high).wait_recv()
                    states_ref[l, high, g] = whole[...] * states_ref[l, high, g] + states_ref[l, h, g]
                return start

            states_ref[l, high, g] = jnp.zeros((modes, LANES), jnp.float32)
            lax.fori_loop(0, highs - 1, join, 0)
            start = [states_ref[l, high, g, pl.ds(i * 8, 8), :] for i in range(eights)]
            scan_blocks(
                blocks, ends_ref.at[g], table(1, g, modes), modes, cols, start, table(3, g, modes)
            )
            if final:
                deliver(g, 1)
                deliver(g, 2)
            else:
                answer(g, 0, half_spans)
            return carry

        lax.fori_loop(0, groups, finish, 0)
        if not final:
            stats(l + 1, 0)

        def finish_rest(g, carry):
            if final:
                deliver(g, 0)
                deliver(g, None)
            else:
                answer(g, half_spans, half_spans)
            return carry

        lax.fori_loop(0, groups, finish_rest, 0)
        if not final:
            stats(l + 1, 1)

    def drain(g, carry):
        own_out(g).wait()
        for bit in range(3):
            out_copy(g, bit, near_by[bit]).wait_recv()
            out_copy(g, bit, low).wait_send()

        def one(h, carry):
            @pl.when(h > high)
            def _():
                for l in range(layers):
                    state_copy(l, g, high, h).wait_send()
            return carry

        return lax.fori_loop(1, highs, one, carry)

    for l in range(layers):
        for part_of in range(2):
            for bit in range(3):
                stats_copy(l, part_of, bit, low).wait_send()
    lax.fori_loop(0, groups, drain, 0)


def local(signal, pool_weight, norm_gain, step_size, mode_out, skip_gain):
    fine, channels = signal.shape
    depth, total = pool_weight.shape
    layers, modes, _ = mode_out.shape
    own_rows = fine // POOL
    rows = own_rows * SPLIT
    width = total // SPLIT
    groups = width // LANES
    highs = lax.axis_size("tm") // SPLIT
    cuts = 2 if depth % 64 == 0 else 1
    dma = pltpu.SemaphoreType.DMA
    vmem, f32, b16 = pltpu.VMEM, jnp.float32, jnp.bfloat16
    anywhere = pl.BlockSpec(memory_space=pl.ANY)
    far = pl.BlockSpec(memory_space=pltpu.HBM)
    return pl.pallas_call(
        functools.partial(section_kernel, highs),
        out_shape=jax.ShapeDtypeStruct((own_rows, total), b16),
        in_specs=[far] * 6,
        out_specs=anywhere,
        scratch_shapes=[
            vmem((fine, channels), b16),
            vmem((rows, POOL * channels), b16),
            vmem((POOL * channels, width), b16),
            vmem((groups, rows, LANES), f32),
            vmem((groups, rows, LANES), f32),
            vmem((groups, rows, LANES), f32),
            vmem((groups, (modes + PAD) * (rows // BLOCK), LANES), f32),
            vmem((layers, 6 * modes, width), f32),
            vmem((layers, width), f32),
            vmem((layers, width), f32),
            vmem((layers, modes, width), f32),
            vmem((layers, width), f32),
            vmem((layers, 2, SPLIT, 8, LANES), f32),
            vmem((layers, groups, modes, LANES), f32),
            vmem((layers, highs, groups, modes, LANES), f32),
            vmem((groups, rows, LANES), b16),
            [
                dma((3, 2, cuts)), dma((3, 2, cuts)), dma((6 + groups,)),
                dma((2, highs, SPLIT, cuts)), dma((highs, SPLIT, cuts)),
                dma((highs, SPLIT, cuts)), dma((highs, SPLIT, cuts)),
                dma((3, PIECES)), dma((3, PIECES)),
                dma((layers, 2, 3)), dma((layers, 2, 3)), dma((layers, highs, groups)),
                dma((layers, highs, groups)), dma((groups, 3)), dma((groups, 3)), dma((2,)), dma((2,)),
            ],
        ],
        compiler_params=pltpu.CompilerParams(
            collective_id=0, has_side_effects=True, vmem_limit_bytes=57000000
        ),
    )(signal, pool_weight, norm_gain, step_size, mode_out, skip_gain)


def solution(mesh):
    placed = (P(("parts", "tm"), None), P("tm", None), P(), P(), P(), P())
    return jax.shard_map(
        local, mesh=mesh, in_specs=placed, out_specs=P(("parts", "tm"), None), check_vma=False
    )
```

```python
import functools

import jax
import jax.numpy as jnp
from jax import lax
from jax.experimental import pallas as pl
from jax.experimental.pallas import tpu as pltpu
from jax.sharding import PartitionSpec as P

POOL = 4
SPLIT = 4
BLOCK = 16
LANES = 128
PIECES = 4
PAD = 1


def block_ends(x_ref, decay_ref, ends_ref, modes, cols, first, count):
    blocks = x_ref.shape[0] // BLOCK
    span = 8 * BLOCK
    pitch = ends_ref.shape[0] // blocks

    def group(g, carry):
        base = pl.multiple_of(g * span, span)
        xs = [x_ref[pl.ds(base + j, 8, stride=BLOCK), cols] for j in range(BLOCK)]
        for n in range(modes):
            decay = jnp.broadcast_to(decay_ref[pl.ds(n, 1), cols], (8, LANES))
            end = xs[0]
            for j in range(1, BLOCK):
                end = end * decay + xs[j]
            ends_ref[pl.ds(g * 8 * pitch + n, 8, stride=pitch), cols] = end
        return carry

    lax.fori_loop(first, first + count, group, 0)


def scan_blocks(blocks, ends_ref, step_ref, modes, cols, start, out_ref=None):
    pitch = ends_ref.shape[0] // blocks
    groups = modes // 8
    steps = [step_ref[pl.ds(i * 8, 8), cols] for i in range(groups)]
    outs = [out_ref[pl.ds(i * 8, 8), cols] for i in range(groups)] if out_ref is not None else None
    states = list(start)
    for b in range(blocks):
        for i in range(groups):
            where = pl.ds(b * pitch + i * 8, 8)
            end = ends_ref[where, cols]
            if outs is not None:
                ends_ref[where, cols] = states[i] * outs[i]
            states[i] = states[i] * steps[i] + end
    return states


def respond(
    x_ref, hidden_ref, ends_ref, powers_ref, kernel_ref, result_ref, modes, cols, first, count
):
    blocks = x_ref.shape[0] // BLOCK
    span = 8 * BLOCK
    pitch = ends_ref.shape[0] // blocks

    def group(g, carry):
        base = pl.multiple_of(g * span, span)
        coefs = [ends_ref[pl.ds(g * 8 * pitch + n, 8, stride=pitch), cols] for n in range(modes)]
        xs = [x_ref[pl.ds(base + j, 8, stride=BLOCK), cols] for j in range(BLOCK)]
        for j in range(BLOCK):
            power = jnp.broadcast_to(powers_ref[pl.ds(j, 1), cols], (8, LANES))
            total = coefs[modes - 1]
            for n in range(modes - 2, -1, -1):
                total = total * power + coefs[n]
            total = total * power
            for i in range(j + 1):
                total = total + xs[i] * jnp.broadcast_to(
                    kernel_ref[pl.ds(j - i, 1), cols], (8, LANES)
                )
            where = pl.ds(base + j, 8, stride=BLOCK)
            gelu = 0.5 * total * (1.0 + lax.erf(total * 0.7071067811865476))
            result_ref[where, cols] = hidden_ref[where, cols] + gelu
        return carry

    lax.fori_loop(first, first + count, group, 0)


MESH = pl.DeviceIdType.MESH


def decay_left(y):
    small = jnp.ones_like(y)
    for k in range(10, 1, -1):
        small = 1.0 - y * (1.0 / k) * small
    return jnp.where(y < 0.5, y * small, 1.0 - jnp.exp(-y))


def make_tables(l, cols, rows, step_ref, mix_ref, skip_ref, table_ref):
    modes = mix_ref.shape[1]
    step = step_ref[pl.ds(l, 1), cols]
    order = lax.broadcasted_iota(jnp.int32, (modes, LANES), 0).astype(jnp.float32) + 1.0
    rates = jnp.broadcast_to(step, (modes, LANES)) * order
    out = mix_ref[l, :, cols] * jnp.sqrt(decay_left(2.0 * rates))
    table_ref[l, pl.ds(0, modes), cols] = jnp.exp(-rates)
    table_ref[l, pl.ds(modes, modes), cols] = jnp.exp(-rates * BLOCK)
    table_ref[l, pl.ds(2 * modes, modes), cols] = jnp.exp(-rates * rows)
    table_ref[l, pl.ds(3 * modes, modes), cols] = out
    lags = lax.broadcasted_iota(jnp.int32, (BLOCK, LANES), 0).astype(jnp.float32) + 1.0
    table_ref[l, pl.ds(4 * modes, BLOCK), cols] = jnp.exp(-lags * jnp.broadcast_to(step, (BLOCK, LANES)))
    skip = skip_ref[pl.ds(l, 1), cols]
    for j in range(BLOCK):
        terms = out * jnp.exp(-float(j) * rates) if j else out
        line = jnp.sum(terms, axis=0, keepdims=True)
        table_ref[l, pl.ds(5 * modes + j, 1), cols] = line if j else line + skip


def section_kernel(
    highs, signal_ref, weight_ref, gain_in, step_in, mix_in, skip_in, out_ref,
    raw_ref, all_ref, cols_ref, first_ref, hidden_ref, x_ref, ends_ref, table_ref,
    gain_ref, step_ref, mix_ref, skip_ref, stats_ref, last_ref, states_ref, rounded_ref, sems
):
    part, place = lax.axis_index("parts"), lax.axis_index("tm")
    high, low = place // SPLIT, place % SPLIT
    depth, width = weight_ref.shape[0], cols_ref.shape[1]
    fine, channels = signal_ref.shape
    half = depth // 2
    cuts = 2 if half % 32 == 0 else 1
    sizes = (half * 3 // 8 // 16 * 16, half - half * 3 // 8 // 16 * 16) if cuts == 2 else (half,)
    starts = (0, sizes[0])
    own_rows = fine // POOL
    rows = own_rows * SPLIT
    piece = own_rows // PIECES
    chunk = SPLIT * depth
    groups = width // LANES
    layers, modes = mix_ref.shape[0], mix_ref.shape[1]
    blocks = rows // BLOCK
    last_step = highs - 1
    other = 1 - part
    exact = lax.Precision.HIGHEST
    (near_send, near_recv, own_sem, line_send, line_recv, side_send, side_recv, rows_send, rows_recv,
     stats_send, stats_recv, state_send, state_recv, out_send, out_recv, extra_send, extra_recv) = sems
    flip = lambda bit: low + bit - 2 * bit * ((low // bit) % 2)
    core, cross, diagonal = flip(1), flip(2), SPLIT - 1 - low
    near_by = (core, cross, diagonal)
    queue = (low, core, cross, diagonal)
    at = lambda p, h, l: (p, h * SPLIT + l)
    own_cols = pl.ds(pl.multiple_of(low * width, width), width)

    own_copies = [
        pltpu.make_async_copy(signal_ref, raw_ref, own_sem.at[0]),
        pltpu.make_async_copy(
            weight_ref.at[:, own_cols],
            cols_ref.at[pl.ds(pl.multiple_of(high * chunk + low * depth, depth), depth), :],
            own_sem.at[1],
        ),
        pltpu.make_async_copy(gain_in.at[:, own_cols], gain_ref, own_sem.at[2]),
        pltpu.make_async_copy(step_in.at[:, own_cols], step_ref, own_sem.at[3]),
        pltpu.make_async_copy(mix_in.at[:, :, own_cols], mix_ref, own_sem.at[4]),
        pltpu.make_async_copy(skip_in.at[:, own_cols], skip_ref, own_sem.at[5]),
    ]
    for copy in own_copies:
        copy.start()

    barrier = pltpu.get_barrier_semaphore()

    def greet(device):
        pl.semaphore_signal(barrier, inc=1, device_id=device, device_id_type=MESH)

    for who in near_by:
        greet(at(part, high, who))
    greet(at(other, high, low))

    def greet_high(h, carry):
        pl.when(h != high)(lambda: greet(at(part, h, low)))
        return carry

    pl.when(high > 0)(lambda: greet(at(part, high - 1, low)))
    pl.when(high < highs - 1)(lambda: greet(at(part, high + 1, low)))
    pl.semaphore_wait(barrier, 4 + jnp.minimum(high, 1) + jnp.minimum(highs - 1 - high, 1))

    def spot(h, l, which, c):
        start = pl.multiple_of(h * chunk + l * depth + which * half + starts[c], 16)
        return cols_ref.at[pl.ds(start, sizes[c]), :]

    def source(to, which, c):
        return weight_ref.at[
            pl.ds(pl.multiple_of(which * half + starts[c], 16), sizes[c]),
            pl.ds(pl.multiple_of(to * width, width), width),
        ]

    def near(bit, which, c):
        to = near_by[bit]
        return pltpu.make_async_remote_copy(
            source(to, which, c), spot(high, low, which, c), near_send.at[bit, which, c],
            near_recv.at[bit, which, c], device_id=at(part, high, to), device_id_type=MESH,
        )

    def near_arrived(bit, which, c):
        where = spot(high, near_by[bit], which, c)
        pltpu.make_async_remote_copy(
            where, where, near_send.at[bit, which, c], near_recv.at[bit, which, c],
            device_id=at(part, high, near_by[bit]), device_id_type=MESH,
        ).wait_recv()

    def line(up, h, l, c, own=False):
        to = jnp.clip(high + (1 if up else -1), 0, highs - 1)
        return pltpu.make_async_remote_copy(
            source(low, part, c) if own else spot(h, l, part, c), spot(h, l, part, c),
            line_send.at[int(up), h, l, c], line_recv.at[h, l, c],
            device_id=at(part, to, low), device_id_type=MESH,
        )

    def both_ways(l, c, own=False):
        pl.when(high < highs - 1)(lambda: line(True, high, l, c, own).start())
        pl.when(high > 0)(lambda: line(False, high, l, c, own).start())

    def side(h, l, which, c):
        return pltpu.make_async_remote_copy(
            spot(h, l, which, c), spot(h, l, which, c), side_send.at[h, l, c], side_recv.at[h, l, c],
            device_id=at(other, high, low), device_id_type=MESH,
        )

    def block(owner, p):
        start = pl.multiple_of(owner * own_rows + p * piece, piece)
        return all_ref.at[pl.ds(start, piece), :]

    def give(bit, p):
        return pltpu.make_async_remote_copy(
            block(low, p), block(low, p), rows_send.at[bit, p], rows_recv.at[bit, p],
            device_id=at(part, high, near_by[bit]), device_id_type=MESH,
        )

    def taken(bit, p):
        where = block(near_by[bit], p)
        pltpu.make_async_remote_copy(
            where, where, rows_send.at[bit, p], rows_recv.at[bit, p],
            device_id=at(part, high, core), device_id_type=MESH,
        ).wait_recv()

    def pass_on(p):
        return pltpu.make_async_remote_copy(
            block(cross, p), block(cross, p), rows_send.at[2, p], rows_recv.at[2, p],
            device_id=at(part, high, core), device_id_type=MESH,
        )

    for c in range(cuts):
        both_ways(low, c, True)
    for bit in (1, 2, 0):
        for c in range(cuts):
            near(bit, part, c).start()
    near(2, other, cuts - 1).start()

    own_copies[0].wait()
    line_of = lax.broadcasted_iota(jnp.int32, (own_rows, fine), 0)
    tick = lax.broadcasted_iota(jnp.int32, (own_rows, fine), 1)
    own_start = pl.multiple_of(low * own_rows, own_rows)
    for q in range(POOL):
        pick = (tick == POOL * line_of + q).astype(jnp.bfloat16)
        picked = jnp.dot(pick, raw_ref[...], preferred_element_type=jnp.float32)
        all_ref[pl.ds(own_start, own_rows), pl.ds(q * channels, channels)] = picked.astype(jnp.bfloat16)

    for p in range(PIECES):
        give(1, p).start()
    for p in range(PIECES):
        give(0, p).start()
    for bit in (1, 2, 0):
        for c in range(cuts if bit != 2 else cuts - 1):
            near(bit, other, c).start()
    for c in range(cuts):
        near_arrived(0, part, c)
        both_ways(core, c)

    for copy in own_copies[1:]:
        copy.wait()

    def lanes(g):
        return pl.ds(pl.multiple_of(g * LANES, LANES), LANES)

    def tables_of(l):
        def one(g, carry):
            make_tables(l, lanes(g), rows, step_ref, mix_ref, skip_ref, table_ref)
            return carry

        lax.fori_loop(0, groups, one, 0)

    tables_of(0)

    def by_side(h, k, c):
        if k == SPLIT - 1 and c == cuts - 1:
            return (h > 0) & (h < highs - 1)
        return True

    def extra(up):
        h = 0 if up else highs - 1
        to = jnp.clip(high + (1 if up else -1), 0, highs - 1)
        where = spot(h, diagonal, other, cuts - 1)
        return pltpu.make_async_remote_copy(
            where, where, extra_send.at[int(up)], extra_recv.at[int(up)],
            device_id=at(part, to, low), device_id_type=MESH,
        )

    def incoming(s):
        return (
            (True, high - s, high - s >= 0, high < highs - 1),
            (False, high + s, high + s < highs, high > 0),
        )

    def arrive(s, k, c):
        for up, h, there, _ in incoming(s):
            @pl.when(there)
            def _(up=up, h=h):
                line(up, h, queue[k], c).wait_recv()
                side(h, queue[k], part, c).start()

    def forward(s, k, c):
        for up, h, there, more in incoming(s):
            pl.when(there & more)(lambda: line(up, h, queue[k], c).start())

    def relay(s, k, c):
        for up, h, there, more in incoming(s):
            @pl.when(there)
            def _(up=up, h=h, more=more):
                line(up, h, queue[k], c).wait_recv()
                pl.when(more)(lambda: line(up, h, queue[k], c).start())
                if by_side(h, k, c) is True:
                    side(h, queue[k], part, c).start()
                else:
                    inner = by_side(h, k, c)
                    pl.when(inner)(lambda: side(h, queue[k], part, c).start())

                    @pl.when(jnp.logical_not(inner))
                    def _():
                        extra(up).wait_recv()
                        pl.when(more)(lambda: extra(up).start())

    def rows_on(p):
        taken(1, p)
        pass_on(p).start()

    for c in range(cuts):
        arrive(1, 0, c)
    for c in range(cuts):
        near_arrived(1, part, c)
        both_ways(cross, c)
        arrive(1, 1, c)
    for c in range(cuts):
        near_arrived(2, part, c)
        both_ways(diagonal, c)
    for k in (0, 1):
        for c in range(cuts):
            forward(1, k, c)
    for c in range(cuts):
        relay(1, 2, c)
    near_arrived(2, other, cuts - 1)
    pl.when(high == 0)(lambda: extra(True).start())
    pl.when(high == highs - 1)(lambda: extra(False).start())
    for layer in range(1, layers):
        tables_of(layer)
    for c in range(cuts):
        relay(1, 3, c)
    rows_on(0)

    def step(s, carry):
        for k in (0, 1):
            for c in range(cuts):
                relay(s, k, c)
        pl.when(s == 2)(lambda: rows_on(1))
        for k in (2, 3):
            for c in range(cuts):
                relay(s, k, c)
        pl.when(s == 2)(lambda: rows_on(2))
        return carry

    lax.fori_loop(2, last_step, step, 0)

    def multiply(start, size):
        start = pl.multiple_of(start, size)
        return jnp.dot(
            all_ref[:, pl.ds(start, size)], cols_ref[pl.ds(start, size), :],
            preferred_element_type=jnp.float32,
        )

    def keep(value, fresh):
        for g in range(groups):
            piece_of = value[:, g * LANES : (g + 1) * LANES]
            first_ref[g] = piece_of if fresh else first_ref[g] + piece_of

    def side_arrived(h, k):
        for c in range(cuts):
            if by_side(h, k, c) is True:
                side(h, queue[k], other, c).wait_recv()
            else:
                pl.when(by_side(h, k, c))(lambda: side(h, queue[k], other, c).wait_recv())

    def add(s, carry):
        for h, there in ((high - s, high - s >= 0), (high + s, high + s < highs)):
            @pl.when(there)
            def _(h=h):
                for k in range(SPLIT):
                    side_arrived(h, k)
                keep(multiply(h * chunk, chunk), False)

        return carry

    def add_each(s, carry):
        if depth % LANES:
            return add(s, carry)

        for h, there in ((high - s, high - s >= 0), (high + s, high + s < highs)):
            @pl.when(there)
            def _(h=h):
                for k in range(SPLIT):
                    side_arrived(h, k)
                    keep(multiply(h * chunk + queue[k] * depth, depth), False)

        return carry

    for k in (0, 1):
        for c in range(cuts):
            relay(last_step, k, c)
    rows_on(3)
    relay(last_step, 2, 0)
    first_ref[...] = jnp.zeros_like(first_ref)
    for p in range(PIECES):
        taken(0, p)
        taken(2, p)
    add(1, 0)
    for c in range(1, cuts):
        relay(last_step, 2, c)
    at_end = (high == 0) | (high == highs - 1)

    @pl.when(at_end)
    def _():
        lax.fori_loop(2, last_step, add, 0)

    for c in range(cuts):
        relay(last_step, 3, c)
    for bit in range(3):
        for c in range(cuts if bit != 2 else cuts - 1):
            near_arrived(bit, other, c)
    keep(multiply(high * chunk, chunk), False)

    @pl.when(jnp.logical_not(at_end))
    def _():
        lax.fori_loop(2, last_step, add_each, 0)

    add_each(last_step, 0)

    def pool_sent():
        for bit in range(3):
            for c in range(cuts):
                near(bit, 0, c).wait_send()
                near(bit, 1, c).wait_send()
        for p in range(PIECES):
            give(0, p).wait_send()
            give(1, p).wait_send()
            pass_on(p).wait_send()

        def sent(h, carry):
            for k, l in enumerate(queue):
                for c in range(cuts):
                    pl.when((h <= high) & (high < highs - 1))(lambda: line(True, h, l, c).wait_send())
                    pl.when((h >= high) & (high > 0))(lambda: line(False, h, l, c).wait_send())
                    pl.when((h != high) & by_side(h, k, c))(lambda: side(h, l, part, c).wait_send())
            return carry

        lax.fori_loop(0, highs, sent, 0)
        pl.when(high < highs - 1)(lambda: extra(True).wait_send())
        pl.when(high > 0)(lambda: extra(False).wait_send())

    def stats_copy(l, part_of, bit, owner):
        return pltpu.make_async_remote_copy(
            stats_ref.at[l, part_of, owner], stats_ref.at[l, part_of, owner],
            stats_send.at[l, part_of, bit], stats_recv.at[l, part_of, bit],
            device_id=at(part, high, near_by[bit]), device_id_type=MESH,
        )

    def state_copy(l, g, origin, target):
        return pltpu.make_async_remote_copy(
            last_ref.at[l, g], states_ref.at[l, origin, g], state_send.at[l, target, g],
            state_recv.at[l, origin, g], device_id=at(part, target, low), device_id_type=MESH,
        )

    def out_cols(owner, g):
        return pl.ds(pl.multiple_of(owner * width + g * LANES, LANES), LANES)

    def out_copy(g, bit, owner):
        start = pl.multiple_of(near_by[bit] * own_rows, own_rows)
        return pltpu.make_async_remote_copy(
            rounded_ref.at[g, pl.ds(start, own_rows), :], out_ref.at[:, out_cols(owner, g)],
            out_send.at[g, bit], out_recv.at[g, bit],
            device_id=at(part, high, near_by[bit]), device_id_type=MESH,
        )

    def own_out(g):
        return pltpu.make_async_copy(
            rounded_ref.at[g, pl.ds(own_start, own_rows), :], out_ref.at[:, out_cols(low, g)], own_sem.at[6 + g]
        )

    spans = rows // (2 * LANES)
    half_rows = spans * LANES
    sub = lax.broadcasted_iota(jnp.int32, (2 * spans, LANES), 0)
    state_of = lambda l: first_ref if l == 0 else hidden_ref

    def fold(wide):
        folded = wide[:, 0:LANES]
        for i in range(1, spans):
            folded = jnp.where(sub % spans == i, wide[:, i * LANES : (i + 1) * LANES], folded)
        return folded

    def stats(l, part_of):
        source_ref = state_of(l)
        rows_of = pl.ds(part_of * half_rows, half_rows)
        values = [source_ref[g, rows_of, :] for g in range(groups)]
        total = values[0]
        for value in values[1:]:
            total = total + value
        mean = jnp.sum(total, axis=-1, keepdims=True) / width
        square = jnp.square(values[0] - mean)
        for value in values[1:]:
            square = square + jnp.square(value - mean)
        ones = jnp.ones((2 * spans, LANES), jnp.float32)
        across = lambda v: lax.dot_general(
            ones, v, (((1,), (1,)), ((), ())), precision=exact, preferred_element_type=jnp.float32
        )
        folded = jnp.where(sub < spans, fold(across(total)) / width, fold(across(square)))
        stats_ref[l, part_of, low, pl.ds(0, 2 * spans), :] = folded
        for bit in (1, 2, 0):
            stats_copy(l, part_of, bit, low).start()

    def moments(l, part_of):
        for bit in range(3):
            stats_copy(l, part_of, bit, near_by[bit]).wait_recv()
        every = [stats_ref[l, part_of, i, pl.ds(0, 2 * spans), :] for i in range(SPLIT)]
        means = [e[0:spans] for e in every]
        row_mean = (means[0] + means[1] + means[2] + means[3]) / SPLIT
        row_var = sum(e[spans : 2 * spans] + width * jnp.square(e[0:spans] - row_mean) for e in every)
        row_scale = lax.rsqrt(row_var / (width * SPLIT) + 1e-05)
        return jnp.transpose(jnp.concatenate([row_mean, row_scale] * (8 // (2 * spans)), axis=0))

    def normalize(l, part_of, both, g):
        gain = gain_ref[pl.ds(l, 1), lanes(g)]
        for i in range(spans):
            where = pl.ds(part_of * half_rows + i * LANES, LANES)
            x_ref[g, where, :] = (
                (state_of(l)[g, where, :] - both[:, i : i + 1]) * both[:, spans + i : spans + i + 1] * gain
            )

    stats(0, 0)
    stats(0, 1)
    pool_sent()

    for l in range(layers):
        source_ref = state_of(l)
        final = l == layers - 1
        whole_spans = rows // (8 * BLOCK)
        half_spans = whole_spans // 2

        def table(index, g, size):
            return table_ref.at[l, pl.ds(index * modes, size), lanes(g)]

        cols = slice(None)
        eights = modes // 8

        def send(g):
            def one(h, carry):
                pl.when(h > high)(lambda: state_copy(l, g, high, h).start())
                return carry

            lax.fori_loop(1, highs, one, 0)

        both = moments(l, 0)
        for g in range(groups):
            normalize(l, 0, both, g)

        def ends_first(g, carry):
            block_ends(
                x_ref.at[g], table(0, g, modes), ends_ref.at[g], modes, cols, 0, half_spans
            )
            return carry

        lax.fori_loop(0, groups, ends_first, 0)
        both = moments(l, 1)
        for g in range(groups):
            normalize(l, 1, both, g)

        def ends(g, carry):
            block_ends(
                x_ref.at[g], table(0, g, modes), ends_ref.at[g], modes, cols, half_spans, half_spans
            )
            zero = [jnp.zeros((8, LANES), jnp.float32)] * eights
            last = scan_blocks(blocks, ends_ref.at[g], table(1, g, modes), modes, cols, zero)
            for i in range(eights):
                last_ref[l, g, pl.ds(i * 8, 8), :] = last[i]
            send(g)
            return carry

        lax.fori_loop(0, groups, ends, 0)

        def answer(g, first, count):
            respond(
                x_ref.at[g], source_ref.at[g], ends_ref.at[g], table(4, g, BLOCK),
                table(5, g, BLOCK), hidden_ref.at[g], modes, cols, first, count,
            )

        def deliver(g, bit):
            owner = low if bit is None else near_by[bit]
            answer(g, owner * (whole_spans // SPLIT), whole_spans // SPLIT)
            where = pl.ds(pl.multiple_of(owner * own_rows, own_rows), own_rows)
            rounded_ref[g, where, :] = hidden_ref[g, where, :].astype(jnp.bfloat16)
            (own_out(g) if bit is None else out_copy(g, bit, low)).start()

        def finish(g, carry):
            whole = table(2, g, modes)

            def join(h, start):
                @pl.when(h < high)
                def _():
                    state_copy(l, g, h, high).wait_recv()
                    states_ref[l, high, g] = whole[...] * states_ref[l, high, g] + states_ref[l, h, g]
                return start

            states_ref[l, high, g] = jnp.zeros((modes, LANES), jnp.float32)
            lax.fori_loop(0, highs - 1, join, 0)
            start = [states_ref[l, high, g, pl.ds(i * 8, 8), :] for i in range(eights)]
            scan_blocks(
                blocks, ends_ref.at[g], table(1, g, modes), modes, cols, start, table(3, g, modes)
            )
            if final:
                deliver(g, 2)
                deliver(g, 1)
            else:
                answer(g, 0, half_spans)
            return carry

        lax.fori_loop(0, groups, finish, 0)
        if not final:
            stats(l + 1, 0)

        def finish_rest(g, carry):
            if final:
                deliver(g, 0)
                deliver(g, None)
            else:
                answer(g, half_spans, half_spans)
            return carry

        lax.fori_loop(0, groups, finish_rest, 0)
        if not final:
            stats(l + 1, 1)

    def drain(g, carry):
        own_out(g).wait()
        for bit in range(3):
            out_copy(g, bit, near_by[bit]).wait_recv()
            out_copy(g, bit, low).wait_send()

        def one(h, carry):
            @pl.when(h > high)
            def _():
                for l in range(layers):
                    state_copy(l, g, high, h).wait_send()
            return carry

        return lax.fori_loop(1, highs, one, carry)

    for l in range(layers):
        for part_of in range(2):
            for bit in range(3):
                stats_copy(l, part_of, bit, low).wait_send()
    lax.fori_loop(0, groups, drain, 0)


def local(signal, pool_weight, norm_gain, step_size, mode_out, skip_gain):
    fine, channels = signal.shape
    depth, total = pool_weight.shape
    layers, modes, _ = mode_out.shape
    own_rows = fine // POOL
    rows = own_rows * SPLIT
    width = total // SPLIT
    groups = width // LANES
    highs = lax.axis_size("tm") // SPLIT
    cuts = 2 if depth % 64 == 0 else 1
    dma = pltpu.SemaphoreType.DMA
    vmem, f32, b16 = pltpu.VMEM, jnp.float32, jnp.bfloat16
    anywhere = pl.BlockSpec(memory_space=pl.ANY)
    far = pl.BlockSpec(memory_space=pltpu.HBM)
    return pl.pallas_call(
        functools.partial(section_kernel, highs),
        out_shape=jax.ShapeDtypeStruct((own_rows, total), b16),
        in_specs=[far] * 6,
        out_specs=anywhere,
        scratch_shapes=[
            vmem((fine, channels), b16),
            vmem((rows, POOL * channels), b16),
            vmem((POOL * channels, width), b16),
            vmem((groups, rows, LANES), f32),
            vmem((groups, rows, LANES), f32),
            vmem((groups, rows, LANES), f32),
            vmem((groups, (modes + PAD) * (rows // BLOCK), LANES), f32),
            vmem((layers, 6 * modes, width), f32),
            vmem((layers, width), f32),
            vmem((layers, width), f32),
            vmem((layers, modes, width), f32),
            vmem((layers, width), f32),
            vmem((layers, 2, SPLIT, 8, LANES), f32),
            vmem((layers, groups, modes, LANES), f32),
            vmem((layers, highs, groups, modes, LANES), f32),
            vmem((groups, rows, LANES), b16),
            [
                dma((3, 2, cuts)), dma((3, 2, cuts)), dma((6 + groups,)),
                dma((2, highs, SPLIT, cuts)), dma((highs, SPLIT, cuts)),
                dma((highs, SPLIT, cuts)), dma((highs, SPLIT, cuts)),
                dma((3, PIECES)), dma((3, PIECES)),
                dma((layers, 2, 3)), dma((layers, 2, 3)), dma((layers, highs, groups)),
                dma((layers, highs, groups)), dma((groups, 3)), dma((groups, 3)), dma((2,)), dma((2,)),
            ],
        ],
        compiler_params=pltpu.CompilerParams(
            collective_id=0, has_side_effects=True, vmem_limit_bytes=57000000
        ),
    )(signal, pool_weight, norm_gain, step_size, mode_out, skip_gain)


def solution(mesh):
    placed = (P(("parts", "tm"), None), P("tm", None), P(), P(), P(), P())
    return jax.shard_map(
        local, mesh=mesh, in_specs=placed, out_specs=P(("parts", "tm"), None), check_vma=False
    )
```
